256 devices in a mesh: team: 2 (over core), row: 16 (over x, y), col: 8 (over z).
Axes of the slice: x: 4, y: 4, z: 8, core: 2. Of those that a mesh axis runs over, the one named last changes fastest.
Arguments:
- front: float32 [2, 12288, 12288], P('team', 'row', 'col')
- row_map: int32 [2, 11264], replicated, may hold values from 0 to 12287, as said below
- tile_owner: int32 [96], replicated, may hold values from 0 to 1
Outputs:
- factor: float32 [2, 12288, 1024], P('team', 'row')
- assembled: float32 [2, 12288, 12288], P('team', 'row', 'col')
The draws below stay inside these ranges and needn't reach their ends.
Inputs may be any that keep to these rules, and one draw needn't show every extreme that they name: row_map[c, i] is the parent row that receives row and column i + 1024 of child c; within one child no parent row appears twice; the 128-row tile of the parent row and the tile of the child row i + 1024 have the same remainder modulo the number of devices along row.
All inputs are finite; a program needn't handle non-finite values.
Results may differ from the reference program's by a relative error of at most 0.0075.
Values may be sent and summed in bfloat16 or wider, within the bound.
A program may use at most 128 MiB of HBM per device.

```python
import jax
import jax.numpy as jnp
from jax import lax

TILE = 128
PANEL = 512
KPAN = 2
RT = 6
F = 12288
CT = 12
M = 11264
N_ROW = 16
N_COL = 8


def draw_front(key, part):
    first_key = jax.random.fold_in(key, 11)
    lead = KPAN * PANEL
    inner = KPAN * PANEL + PANEL
    base = jax.random.normal(first_key, (2, F, inner), jnp.float32)
    scales = jnp.ones((2, F), jnp.float32)
    margin = 0.25
    boost = jnp.where(jnp.arange(F) < lead, 4.0, 1.0).astype(jnp.float32)
    factors = base * (scales * boost[None, :])[:, :, None]
    gram = jnp.einsum('cik,cjk->cij', factors, factors, precision=lax.Precision.HIGHEST) / inner
    identity = jnp.eye(F, dtype=jnp.float32)
    matrix = 0.5 * (gram + jnp.swapaxes(gram, 1, 2)) + margin * identity[None, :, :]
    shaped = matrix.reshape(2, RT, N_ROW, TILE, F)
    matrix = jnp.transpose(shaped, (0, 2, 1, 3, 4)).reshape(2, F, F)
    shaped = matrix.reshape(2, F, CT, N_COL, TILE)
    return jnp.transpose(shaped, (0, 1, 3, 2, 4)).reshape(2, F, F)


def draw_row_map(key, part):
    base_key = jax.random.fold_in(key, 21)
    classes = jnp.arange(N_ROW)
    child_rows = KPAN * PANEL + jnp.arange(M)
    child_tile = child_rows // TILE
    residue = child_tile % N_ROW
    ordinal = child_tile // N_ROW * TILE + child_rows % TILE
    results = []
    for child in range(2):
        child_key = jax.random.fold_in(base_key, child)
        orders = jax.vmap(lambda index: jax.random.permutation(jax.random.fold_in(child_key, index), RT * TILE))(classes)
        placed = orders[residue, ordinal]
        parent_tile = placed // TILE * N_ROW + residue
        results.append((parent_tile * TILE + placed % TILE).astype(jnp.int32))
    return jnp.stack(results)


def with_ends(drawn, key, least, top_value):
    longest = drawn.shape.index(max(drawn.shape))
    spots = []
    for shift in (0, 1):
        where = [jax.random.randint(jax.random.fold_in(key, axis), (), 0, length) for axis, length in enumerate(drawn.shape)]
        where[longest] = (where[longest] + shift) % drawn.shape[longest]
        spots.append(tuple(where))
    return drawn.at[spots[0]].set(least).at[spots[1]].set(top_value)


def setup_inputs(seed: int = 0) -> dict:
    keys = jax.random.split(jax.random.key(seed), 4)
    front = draw_front(jax.random.fold_in(keys[3], 71), 0)
    row_map = draw_row_map(jax.random.fold_in(keys[3], 71), 0)
    tile_owner = with_ends(jax.random.randint(keys[2], (F // TILE,), 0, 2), jax.random.fold_in(keys[2], 1), 0, 1).astype(jnp.int32)
    return dict(front=front, row_map=row_map, tile_owner=tile_owner)


def rows_natural(stored):
    width = stored.shape[2]
    shaped = stored.reshape(2, N_ROW, RT, TILE, width)
    return jnp.transpose(shaped, (0, 2, 1, 3, 4)).reshape(2, F, width)

def rows_stored(natural):
    width = natural.shape[2]
    shaped = natural.reshape(2, RT, N_ROW, TILE, width)
    return jnp.transpose(shaped, (0, 2, 1, 3, 4)).reshape(2, F, width)

def cols_natural(stored):
    shaped = stored.reshape(2, F, N_COL, CT, TILE)
    return jnp.transpose(shaped, (0, 1, 3, 2, 4)).reshape(2, F, F)

def cols_stored(natural):
    shaped = natural.reshape(2, F, CT, N_COL, TILE)
    return jnp.transpose(shaped, (0, 1, 3, 2, 4)).reshape(2, F, F)

def reference(front, row_map, tile_owner):
    natural = cols_natural(rows_natural(front))
    row_ids = jnp.arange(F)[:, None]
    factors = []
    parent = jnp.zeros((F, F), jnp.float32)
    for child in range(2):
        matrix = natural[child]
        blocks = []
        for panel in range(KPAN):
            low_edge = panel * PANEL
            high_edge = low_edge + PANEL
            panel_strip = matrix[:, low_edge:high_edge]
            lower_factor = jnp.linalg.cholesky(panel_strip[low_edge:high_edge])
            solved = lax.linalg.triangular_solve(lower_factor, panel_strip, left_side=False, lower=True, transpose_a=True)
            blocks.append(jnp.where(row_ids >= low_edge, solved, 0.0))
            used_rows = jnp.where(row_ids >= high_edge, solved, 0.0).astype(jnp.bfloat16)
            matrix = matrix - jnp.dot(used_rows.astype(jnp.float32), used_rows.T.astype(jnp.float32), preferred_element_type=jnp.float32)
        factors.append(jnp.concatenate(blocks, axis=1))
        start = KPAN * PANEL
        update_part = matrix[start:, start:].astype(jnp.bfloat16)
        targets = row_map[child].astype(jnp.int32)
        parent = parent.at[targets[:, None], targets[None, :]].add(update_part.astype(jnp.float32))
    owner_rows = tile_owner[jnp.arange(F) // TILE]
    assembled = jnp.stack([jnp.where((owner_rows == team_id)[:, None], parent, 0.0) for team_id in range(2)])
    factor_out = rows_stored(jnp.stack(factors))
    return (factor_out, cols_stored(rows_stored(assembled)))
```

```python
import jax
import jax.numpy as jnp
from jax import lax
from jax.experimental import pallas as pl
from jax.experimental.pallas import tpu as pltpu
from jax.sharding import PartitionSpec as P

T = 128
LEAD = 1024
NB = 8
RT = 6
CT = 12
ROWS = RT * T
COLS = CT * T
NZ = 8
ND = 5
MESH = pl.DeviceIdType.MESH
VMEM_LIMIT = 60 << 20
F32 = jnp.float32
BF16 = jnp.bfloat16
NN = (((1,), (0,)), ((), ()))
NT = (((1,), (1,)), ((), ()))
TN = (((0,), (0,)), ((), ()))


def dot1(a, b, dims):
    return lax.dot_general(a, b, dims, preferred_element_type=F32)


def split(a):
    hi = a.astype(BF16)
    return hi, (a - hi.astype(F32)).astype(BF16)


def dot3(a, b, dims):
    ah, al = split(a)
    bh, bl = split(b)
    return dot1(ah, bh, dims) + dot1(ah, bl, dims) + dot1(al, bh, dims)


def row_of(x, y):
    return y + jnp.where((x == 0) | (x == 3), 0, 4)


def gather_kernel(front, ga, gb, ra, rb, zs, rows_f, rows_b, tile, half, rhalf,
                  lsem, s0, r0, sz, rz, sp, rp, sq, rq, sr, rr):
    pos = lax.axis_index("row")
    z = lax.axis_index("col")
    x, y = pos // 4, pos % 4
    xs = lambda d: ((x + d) % 4) * 4 + y
    ys = lambda d: x * 4 + (y + d) % 4
    row = row_of(x, y)

    c_col = pltpu.make_async_copy(front.at[0, :, pl.ds(0, T)], zs.at[z], lsem.at[0])
    c_row = pltpu.make_async_copy(front.at[0, pl.ds(0, T), :], rows_f, lsem.at[1])
    c_tile = pltpu.make_async_copy(front.at[0, pl.ds(0, T), pl.ds(0, T)], tile, lsem.at[2])
    c_half = pltpu.make_async_copy(front.at[0, pl.ds(0, 64), pl.ds(0, T)], half, lsem.at[3])
    c_tile.start()
    c_row.start()
    c_col.start()

    @pl.when(x < 2)
    def _():
        c_half.start()

    bar = pltpu.get_barrier_semaphore()
    for d in (1, 3):
        pl.semaphore_signal(bar, inc=1, device_id={"row": xs(d)}, device_id_type=MESH)
        pl.semaphore_signal(bar, inc=1, device_id={"row": ys(d)}, device_id_type=MESH)
    for d in range(1, NZ):
        pl.semaphore_signal(bar, inc=1, device_id={"col": (z + d) % NZ}, device_id_type=MESH)
    c_row.wait()
    rows_b[...] = rows_f[...].astype(BF16)
    c_tile.wait()
    c_col.wait()

    @pl.when(x < 2)
    def _():
        c_half.wait()

    pl.semaphore_wait(bar, 4 + NZ - 1)

    mirror = {"row": (3 - x) * 4 + y}
    c0 = pltpu.make_async_remote_copy(tile.at[pl.ds(64, 64)], half, s0.at[0], r0.at[0], device_id=mirror, device_id_type=MESH)
    c1 = pltpu.make_async_remote_copy(rows_b.at[pl.ds(64, 64)], rhalf, s0.at[1], r0.at[1], device_id=mirror, device_id_type=MESH)

    @pl.when(x < 2)
    def _():
        c0.start()
        c1.start()

    def ring(step):
        up, dn = (z - step + 1 + NZ) % NZ, (z + step - 1) % NZ
        if step < 4:
            src_u, src_d = zs.at[up], zs.at[dn]
        else:
            src_u, src_d = zs.at[up, pl.ds(0, ROWS // 2)], zs.at[dn, pl.ds(ROWS // 2, ROWS // 2)]
        a = pltpu.make_async_remote_copy(src_u, src_u, sr.at[0, step - 1], rr.at[0, step - 1], device_id={"col": (z + 1) % NZ}, device_id_type=MESH)
        b = pltpu.make_async_remote_copy(src_d, src_d, sr.at[1, step - 1], rr.at[1, step - 1], device_id={"col": (z + NZ - 1) % NZ}, device_id_type=MESH)
        return a, b

    def ring_recv(step):
        up, dn = (z - step + NZ) % NZ, (z + step) % NZ
        if step < 4:
            dst_u, dst_d = zs.at[up], zs.at[dn]
        else:
            dst_u, dst_d = zs.at[up, pl.ds(0, ROWS // 2)], zs.at[dn, pl.ds(ROWS // 2, ROWS // 2)]
        pltpu.make_async_remote_copy(dst_u, dst_u, sr.at[0, step - 1], rr.at[0, step - 1], device_id={"col": (z + 1) % NZ}, device_id_type=MESH).wait_recv()
        pltpu.make_async_remote_copy(dst_d, dst_d, sr.at[1, step - 1], rr.at[1, step - 1], device_id={"col": (z + NZ - 1) % NZ}, device_id_type=MESH).wait_recv()

    @pl.when(x >= 2)
    def _():
        c0.wait_recv()

    mine = (z - row + NZ) % NZ
    o1 = pltpu.make_async_copy(half.at[pl.ds(0, 32)], ga.at[y, x, jnp.minimum(mine, ND - 1)], lsem.at[4])
    o2 = pltpu.make_async_copy(half.at[pl.ds(32, 32)], gb.at[x, y, jnp.minimum(mine, ND - 1)], lsem.at[5])

    def zsend(k, d):
        slot = jnp.minimum(mine, ND - 1)
        dst = ga.at[y, x, slot] if k == 0 else gb.at[x, y, slot]
        return pltpu.make_async_remote_copy(half.at[pl.ds(32 * k, 32)], dst, sz.at[k, d], rz.at[k, slot], device_id={"col": (z + d) % NZ}, device_id_type=MESH)

    @pl.when(mine < ND)
    def _():
        for d in (4, 3, 5, 2, 6, 1, 7):
            zsend(0, d).start()
            zsend(1, d).start()
        o1.start()
        o2.start()
        o1.wait()
        o2.wait()

    for d in range(ND):
        @pl.when(mine != d)
        def _():
            pltpu.make_async_remote_copy(half.at[pl.ds(0, 32)], ga.at[y, x, d], sz.at[0, 0], rz.at[0, d], device_id={"col": (z + 1) % NZ}, device_id_type=MESH).wait_recv()
            pltpu.make_async_remote_copy(half.at[pl.ds(32, 32)], gb.at[x, y, d], sz.at[1, 0], rz.at[1, d], device_id={"col": (z + 1) % NZ}, device_id_type=MESH).wait_recv()

    ring_copies = list(ring(1))
    for c in ring_copies:
        c.start()

    def plane(buf, first, step, up, ss, rs, cut):
        f, s = (x, y) if first else (y, x)
        fd, sd = (xs, ys) if first else (ys, xs)
        if step <= 2:
            base = lambda d: buf.at[s, (f + d) % 4]
            dev = fd
        else:
            base = lambda d: buf.at[(s + d) % 4]
            dev = sd
        me = step - 1
        if step % 2 == 1:
            src, rcv = base(0), base(3 if up else 1)
        else:
            src, rcv = base(3 if up else 1), base(2)
            src, rcv = cut(src, up, step), cut(rcv, up, step)
        k = 0 if up else 1
        to = {"row": dev(1 if up else 3)}
        send = pltpu.make_async_remote_copy(src, src, ss.at[me, k], rs.at[me, k], device_id=to, device_id_type=MESH)
        recv = pltpu.make_async_remote_copy(rcv, rcv, ss.at[me, k], rs.at[me, k], device_id=to, device_id_type=MESH)
        return send, recv

    def cut_lead(ref, up, step):
        h = pl.ds(0 if up else 16, 16)
        return ref.at[:, h] if step == 2 else ref.at[:, :, h]

    def cut_strip(ref, up, step):
        h = pl.ds(0 if up else 16, 16)
        return ref.at[h] if step == 2 else ref.at[:, h]

    def plane_step(step, bufs, ss, rs, cut):
        out = []
        for part in range(2):
            for up in (True, False):
                out.append(plane(bufs[part], part == 0, step, up, ss.at[part], rs.at[part], cut))
        return out

    done = []
    for step in range(1, 5):
        cs = plane_step(step, (ga, gb), sp, rp, cut_lead)
        for s, _ in cs:
            s.start()
        done += [s for s, _ in cs]
        for _, r in cs:
            r.wait_recv()

    @pl.when(x >= 2)
    def _():
        c1.wait_recv()
        a = pltpu.make_async_copy(rhalf.at[pl.ds(0, 32)], ra.at[y, x], lsem.at[6])
        b = pltpu.make_async_copy(rhalf.at[pl.ds(32, 32)], rb.at[x, y], lsem.at[7])
        a.start()
        b.start()
        a.wait()
        b.wait()

    @pl.when(x < 2)
    def _():
        a = pltpu.make_async_copy(rows_b.at[pl.ds(0, 32)], ra.at[y, x], lsem.at[6])
        b = pltpu.make_async_copy(rows_b.at[pl.ds(32, 32)], rb.at[x, y], lsem.at[7])
        a.start()
        b.start()
        a.wait()
        b.wait()

    for step in range(1, 5):
        cs = plane_step(step, (ra, rb), sq, rq, cut_strip)
        for s, _ in cs:
            s.start()
        done += [s for s, _ in cs]
        ring_recv(step)
        if step < 4:
            nxt = list(ring(step + 1))
            for c in nxt:
                c.start()
            ring_copies += nxt
        for _, r in cs:
            r.wait_recv()

    for c in done + ring_copies:
        c.wait_send()

    @pl.when(x < 2)
    def _():
        c0.wait_send()
        c1.wait_send()

    @pl.when(mine < ND)
    def _():
        for d in range(1, NZ):
            zsend(0, d).wait_send()
            zsend(1, d).wait_send()


def gather(front):
    vm = pl.BlockSpec(memory_space=pltpu.VMEM)
    dma = pltpu.SemaphoreType.DMA
    return pl.pallas_call(
        gather_kernel,
        out_shape=(
            jax.ShapeDtypeStruct((4, 4, ND, 32, T), F32),
            jax.ShapeDtypeStruct((4, 4, ND, 32, T), F32),
            jax.ShapeDtypeStruct((4, 4, 32, COLS), BF16),
            jax.ShapeDtypeStruct((4, 4, 32, COLS), BF16),
            jax.ShapeDtypeStruct((NZ, ROWS, T), F32),
        ),
        in_specs=[pl.BlockSpec(memory_space=pl.ANY)],
        out_specs=(vm,) * 5,
        scratch_shapes=[
            pltpu.VMEM((T, COLS), F32), pltpu.VMEM((T, COLS), BF16), pltpu.VMEM((T, T), F32),
            pltpu.VMEM((64, T), F32), pltpu.VMEM((64, COLS), BF16),
            dma((8,)), dma((2,)), dma((2,)), dma((2, NZ)), dma((2, ND)),
            dma((2, 4, 2)), dma((2, 4, 2)), dma((2, 4, 2)), dma((2, 4, 2)), dma((2, 4)), dma((2, 4)),
        ],
        compiler_params=pltpu.CompilerParams(collective_id=0, has_side_effects=True, vmem_limit_bytes=VMEM_LIMIT),
        name="gather",
    )(front)


def factor_block(block):
    sub = lax.broadcasted_iota(jnp.int32, (8, T), 0)
    lane = lax.broadcasted_iota(jnp.int32, (8, T), 1)
    V = [block[8 * s : 8 * s + 8, :] for s in range(16)]
    W = [jnp.where(lane == sub + 8 * s, 1.0, 0.0).astype(F32) for s in range(16)]
    lb = lambda v, j: jnp.broadcast_to(v[:, j : j + 1], (8, T))
    sb = lambda v, k: jnp.broadcast_to(v[k : k + 1, :], (8, T))
    for t in range(16):
        v, w = V[t], W[t]
        C = [lb(v, 8 * t + j) for j in range(8)]
        rv, rw, rs, uk = [], [], [], []
        for k in range(8):
            r = lax.rsqrt(sb(C[k], k))
            a, b = sb(v, k) * r, sb(w, k) * r
            m = jnp.where(sub > k, C[k] * r, 0.0)
            us = {}
            for j in range(k + 1, 8):
                us[j] = sb(C[j], k) * r
                C[j] = C[j] - m * us[j]
            v = jnp.where(sub == k, a, v - m * a)
            w = jnp.where(sub == k, b, w - m * b)
            rv.append(a)
            rw.append(b)
            rs.append(r)
            uk.append(us)
        V[t], W[t] = v, w
        for s in range(t + 1, 16):
            Cs = [lb(V[s], 8 * t + j) for j in range(8)]
            vs, ws = V[s], W[s]
            for k in range(8):
                m = Cs[k] * rs[k]
                for j in range(k + 1, 8):
                    Cs[j] = Cs[j] - m * uk[k][j]
                vs = vs - m * rv[k]
                ws = ws - m * rw[k]
            V[s], W[s] = vs, ws
    return jnp.concatenate(W, axis=0)


def lead_kernel(ga, gb, u_ref, w_ref):
    for i in range(NB):
        y = i % 4
        top, bot = (0, 3) if i < 4 else (1, 2)
        for d in range(ND):
            j = (i + d) % NB
            if d == 4 and i >= 4:
                continue
            parts = [ga[y, top, d], gb[top, y, d], ga[y, bot, d], gb[bot, y, d]]
            if j >= i:
                for k in range(4):
                    u_ref[i * T + 32 * k : i * T + 32 * k + 32, j * T : j * T + T] = parts[k]
            else:
                u_ref[j * T : j * T + T, i * T : i * T + T] = jnp.concatenate(parts, axis=0).T
    for i in range(1, NB):
        u_ref[i * T : i * T + T, 0 : i * T] = jnp.zeros((T, i * T), F32)
    col = lax.broadcasted_iota(jnp.int32, (T, LEAD), 1)
    sub = lax.broadcasted_iota(jnp.int32, (T, LEAD), 0)

    def body(J, _):
        j0 = pl.multiple_of(J * T, T)
        inv = factor_block(u_ref[pl.ds(j0, T), pl.ds(j0, T)])
        w_ref[J] = inv
        U = dot3(inv, u_ref[pl.ds(j0, T), :], NN)
        u_ref[pl.ds(j0, T), :] = jnp.where(col >= sub + j0, U, 0.0)

        def upd(I, _):
            i0 = pl.multiple_of(I * T, T)
            ui = u_ref[pl.ds(j0, T), pl.ds(i0, T)]
            u_ref[pl.ds(i0, T), :] = u_ref[pl.ds(i0, T), :] - dot3(ui, u_ref[pl.ds(j0, T), :], TN)
            return 0

        lax.fori_loop(J + 1, NB, upd, 0)
        return 0

    lax.fori_loop(0, NB, body, 0)


def lead_factor(ga, gb):
    vm = pl.BlockSpec(memory_space=pltpu.VMEM)
    return pl.pallas_call(
        lead_kernel,
        out_shape=(jax.ShapeDtypeStruct((LEAD, LEAD), F32), jax.ShapeDtypeStruct((NB, T, T), F32)),
        in_specs=[vm, vm],
        out_specs=(vm, vm),
        compiler_params=pltpu.CompilerParams(vmem_limit_bytes=VMEM_LIMIT),
        name="lead",
    )(ga, gb)


def one_hot(rm_ref, team, first, start, out):
    sub = lax.broadcasted_iota(jnp.int32, (ROWS, T), 0)
    for s in range(RT):
        tile = s * 16 + first
        line = rm_ref[team, pl.ds(jnp.maximum(tile - NB, 0), 1), :]
        spot = jnp.where(tile >= NB, (line // 2048) * T + line % T, -1)
        out[:, s * T : s * T + T] = jnp.where(sub == spot, 1.0, 0.0).astype(BF16)


def update_kernel(front, ra, rb, zs, u_ref, w_ref, rm_ref, fac, placed, ub, xb, yb, upd, pr, pe, po):
    team = lax.axis_index("team")
    pos = lax.axis_index("row")
    z = lax.axis_index("col")
    ub[...] = u_ref[...].astype(BF16)
    one_hot(rm_ref, team, pos, 0, pr)
    one_hot(rm_ref, team, z, 0, pe)
    one_hot(rm_ref, team, z + NZ, 0, po)
    r = lax.broadcasted_iota(jnp.int32, (T, T), 0)
    c = lax.broadcasted_iota(jnp.int32, (T, T), 1)
    for J in range(NB):
        cs = slice(J * T, J * T + T)
        acc = zs[J]
        if J:
            acc = acc - dot1(xb[:, : J * T], ub[: J * T, cs], NN)
        xj = dot3(acc, w_ref[J], NT)
        xb[:, cs] = xj.astype(BF16)
        fac[T:, cs] = xj[T:]
        fac[:T, cs] = jnp.where(pos * T + r >= J * T + c, xj[:T], 0.0)

    wide = 512

    def ystep(n, _):
        n0 = pl.multiple_of(n * wide, wide)
        for J in range(NB):
            cs = slice(J * T, J * T + T)
            y = J % 4
            top, bot = (0, 3) if J < 4 else (1, 2)
            parts = [ra[y, top, :, pl.ds(n0, wide)], rb[top, y, :, pl.ds(n0, wide)], ra[y, bot, :, pl.ds(n0, wide)], rb[bot, y, :, pl.ds(n0, wide)]]
            acc = jnp.concatenate(parts, axis=0).astype(F32)
            if J:
                acc = acc - dot1(ub[: J * T, cs], yb[: J * T, pl.ds(n0, wide)], TN)
            yj = dot3(w_ref[J], acc, NN)
            yb[cs, pl.ds(n0, wide)] = yj.astype(BF16)
        return 0

    lax.fori_loop(0, COLS // wide, ystep, 0)

    def ustep(n, _):
        n0 = pl.multiple_of(n * 256, 256)
        upd[:, pl.ds(n0, 256)] = (front[0, :, pl.ds(n0, 256)] - dot1(xb[...], yb[:, pl.ds(n0, 256)], NN)).astype(BF16)
        t = dot1(pr[...], upd[:, pl.ds(n0, 256)], NN).astype(BF16)
        upd[:, pl.ds(n0, 256)] = t
        return 0

    lax.fori_loop(0, COLS // 256, ustep, 0)
    even = jnp.concatenate([upd[:, 2 * s * T : 2 * s * T + T] for s in range(RT)], axis=1)
    odd = jnp.concatenate([upd[:, (2 * s + 1) * T : (2 * s + 2) * T] for s in range(RT)], axis=1)
    for s in range(RT):
        placed[:, 2 * s * T : 2 * s * T + T] = dot1(even, pe[s * T : s * T + T, :], NT).astype(BF16)
        placed[:, (2 * s + 1) * T : (2 * s + 2) * T] = dot1(odd, po[s * T : s * T + T, :], NT).astype(BF16)


def update(front, ra, rb, zs, u, w, rm):
    vm = pl.BlockSpec(memory_space=pltpu.VMEM)
    return pl.pallas_call(
        update_kernel,
        out_shape=(jax.ShapeDtypeStruct((ROWS, LEAD), F32), jax.ShapeDtypeStruct((ROWS, COLS), BF16)),
        in_specs=[vm] * 7,
        out_specs=(vm, vm),
        scratch_shapes=[
            pltpu.VMEM((LEAD, LEAD), BF16), pltpu.VMEM((ROWS, LEAD), BF16), pltpu.VMEM((LEAD, COLS), BF16),
            pltpu.VMEM((ROWS, COLS), BF16), pltpu.VMEM((ROWS, ROWS), BF16), pltpu.VMEM((ROWS, ROWS), BF16), pltpu.VMEM((ROWS, ROWS), BF16),
        ],
        compiler_params=pltpu.CompilerParams(vmem_limit_bytes=VMEM_LIMIT),
        name="update",
    )(front, ra, rb, zs, u, w, rm)


def shards(front, row_map, tile_owner):
    team = lax.axis_index("team")
    pos = lax.axis_index("row")
    ga, gb, ra, rb, zs = gather(front)
    u, w = lead_factor(ga, gb)
    fac, placed = update(front, ra, rb, zs, u, w, row_map.reshape(2, -1, T))
    other = lax.ppermute(placed, "team", [(0, 1), (1, 0)])
    owned = jnp.take(tile_owner, jnp.arange(RT) * 16 + pos) == team
    owned = jnp.repeat(owned, T)
    assembled = jnp.where(owned[:, None], placed.astype(F32) + other.astype(F32), 0.0)
    return fac[None], assembled[None]


def solution(mesh):
    return jax.shard_map(
        shards,
        mesh=mesh,
        in_specs=(P("team", "row", "col"), P(), P()),
        out_specs=(P("team", "row", None), P("team", "row", "col")),
        check_vma=False,
    )
```

```python
import jax
import jax.numpy as jnp
from jax import lax
from jax.experimental import pallas as pl
from jax.experimental.pallas import tpu as pltpu
from jax.sharding import PartitionSpec as P

T = 128
LEAD = 1024
NB = 8
RT = 6
CT = 12
ROWS = RT * T
COLS = CT * T
NZ = 8
ND = 5
MESH = pl.DeviceIdType.MESH
VMEM_LIMIT = 60 << 20
F32 = jnp.float32
BF16 = jnp.bfloat16
NN = (((1,), (0,)), ((), ()))
NT = (((1,), (1,)), ((), ()))
TN = (((0,), (0,)), ((), ()))


def dot1(a, b, dims):
    return lax.dot_general(a, b, dims, preferred_element_type=F32)


def split(a):
    hi = a.astype(BF16)
    return hi, (a - hi.astype(F32)).astype(BF16)


def dot3(a, b, dims):
    ah, al = split(a)
    bh, bl = split(b)
    return dot1(ah, bh, dims) + dot1(ah, bl, dims) + dot1(al, bh, dims)


def row_of(x, y):
    return y + jnp.where((x == 0) | (x == 3), 0, 4)


def panel_kernel(front, u_ref, w_ref, ra, rb, zs, ga, gb, rows_f, rows_b, tile, half, rhalf,
                 lsem, s0, r0, sz, rz, sp, rp, sq, rq, sr, rr):
    pos = lax.axis_index("row")
    z = lax.axis_index("col")
    x, y = pos // 4, pos % 4
    xs = lambda d: ((x + d) % 4) * 4 + y
    ys = lambda d: x * 4 + (y + d) % 4
    row = row_of(x, y)

    c_col = pltpu.make_async_copy(front.at[0, :, pl.ds(0, T)], zs.at[z], lsem.at[0])
    c_row = pltpu.make_async_copy(front.at[0, pl.ds(0, T), :], rows_f, lsem.at[1])
    c_tile = pltpu.make_async_copy(front.at[0, pl.ds(0, T), pl.ds(0, T)], tile, lsem.at[2])
    c_half = pltpu.make_async_copy(front.at[0, pl.ds(0, 64), pl.ds(0, T)], half, lsem.at[3])
    c_tile.start()
    c_row.start()
    c_col.start()

    @pl.when(x < 2)
    def _():
        c_half.start()

    bar = pltpu.get_barrier_semaphore()
    for d in (1, 3):
        pl.semaphore_signal(bar, inc=1, device_id={"row": xs(d)}, device_id_type=MESH)
        pl.semaphore_signal(bar, inc=1, device_id={"row": ys(d)}, device_id_type=MESH)
    for d in range(1, NZ):
        pl.semaphore_signal(bar, inc=1, device_id={"col": (z + d) % NZ}, device_id_type=MESH)
    c_row.wait()
    rows_b[...] = rows_f[...].astype(BF16)
    c_tile.wait()
    c_col.wait()

    @pl.when(x < 2)
    def _():
        c_half.wait()

    pl.semaphore_wait(bar, 4 + NZ - 1)

    mirror = {"row": (3 - x) * 4 + y}
    c0 = pltpu.make_async_remote_copy(tile.at[pl.ds(64, 64)], half, s0.at[0], r0.at[0], device_id=mirror, device_id_type=MESH)
    c1 = pltpu.make_async_remote_copy(rows_b.at[pl.ds(64, 64)], rhalf, s0.at[1], r0.at[1], device_id=mirror, device_id_type=MESH)

    @pl.when(x < 2)
    def _():
        c0.start()
        c1.start()

    def ring(step):
        up, dn = (z - step + 1 + NZ) % NZ, (z + step - 1) % NZ
        if step < 4:
            src_u, src_d = zs.at[up], zs.at[dn]
        else:
            src_u, src_d = zs.at[up, pl.ds(0, ROWS // 2)], zs.at[dn, pl.ds(ROWS // 2, ROWS // 2)]
        a = pltpu.make_async_remote_copy(src_u, src_u, sr.at[0, step - 1], rr.at[0, step - 1], device_id={"col": (z + 1) % NZ}, device_id_type=MESH)
        b = pltpu.make_async_remote_copy(src_d, src_d, sr.at[1, step - 1], rr.at[1, step - 1], device_id={"col": (z + NZ - 1) % NZ}, device_id_type=MESH)
        return a, b

    def ring_recv(step):
        up, dn = (z - step + NZ) % NZ, (z + step) % NZ
        if step < 4:
            dst_u, dst_d = zs.at[up], zs.at[dn]
        else:
            dst_u, dst_d = zs.at[up, pl.ds(0, ROWS // 2)], zs.at[dn, pl.ds(ROWS // 2, ROWS // 2)]
        pltpu.make_async_remote_copy(dst_u, dst_u, sr.at[0, step - 1], rr.at[0, step - 1], device_id={"col": (z + 1) % NZ}, device_id_type=MESH).wait_recv()
        pltpu.make_async_remote_copy(dst_d, dst_d, sr.at[1, step - 1], rr.at[1, step - 1], device_id={"col": (z + NZ - 1) % NZ}, device_id_type=MESH).wait_recv()

    @pl.when(x >= 2)
    def _():
        c0.wait_recv()

    mine = (z - row + NZ) % NZ
    o1 = pltpu.make_async_copy(half.at[pl.ds(0, 32)], ga.at[y, x, jnp.minimum(mine, ND - 1)], lsem.at[4])
    o2 = pltpu.make_async_copy(half.at[pl.ds(32, 32)], gb.at[x, y, jnp.minimum(mine, ND - 1)], lsem.at[5])

    def zsend(k, d):
        slot = jnp.minimum(mine, ND - 1)
        dst = ga.at[y, x, slot] if k == 0 else gb.at[x, y, slot]
        return pltpu.make_async_remote_copy(half.at[pl.ds(32 * k, 32)], dst, sz.at[k, d], rz.at[k, slot], device_id={"col": (z + d) % NZ}, device_id_type=MESH)

    @pl.when(mine < ND)
    def _():
        for d in (4, 3, 5, 2, 6, 1, 7):
            zsend(0, d).start()
            zsend(1, d).start()
        o1.start()
        o2.start()
        o1.wait()
        o2.wait()

    for d in range(ND):
        @pl.when(mine != d)
        def _():
            pltpu.make_async_remote_copy(half.at[pl.ds(0, 32)], ga.at[y, x, d], sz.at[0, 0], rz.at[0, d], device_id={"col": (z + 1) % NZ}, device_id_type=MESH).wait_recv()
            pltpu.make_async_remote_copy(half.at[pl.ds(32, 32)], gb.at[x, y, d], sz.at[1, 0], rz.at[1, d], device_id={"col": (z + 1) % NZ}, device_id_type=MESH).wait_recv()

    for c in ring(1):
        c.start()

    def plane(buf, first, step, up, ss, rs, cut):
        f, s = (x, y) if first else (y, x)
        fd, sd = (xs, ys) if first else (ys, xs)
        if step <= 2:
            base = lambda d: buf.at[s, (f + d) % 4]
            dev = fd
        else:
            base = lambda d: buf.at[(s + d) % 4]
            dev = sd
        me = step - 1
        if step % 2 == 1:
            src, rcv = base(0), base(3 if up else 1)
        else:
            src, rcv = base(3 if up else 1), base(2)
            src, rcv = cut(src, up, step), cut(rcv, up, step)
        k = 0 if up else 1
        to = {"row": dev(1 if up else 3)}
        send = pltpu.make_async_remote_copy(src, src, ss.at[me, k], rs.at[me, k], device_id=to, device_id_type=MESH)
        recv = pltpu.make_async_remote_copy(rcv, rcv, ss.at[me, k], rs.at[me, k], device_id=to, device_id_type=MESH)
        return send, recv

    def cut_lead(ref, up, step):
        h = pl.ds(0 if up else 16, 16)
        return ref.at[:, h] if step == 2 else ref.at[:, :, h]

    def cut_strip(ref, up, step):
        h = pl.ds(0 if up else 16, 16)
        return ref.at[h] if step == 2 else ref.at[:, h]

    def plane_step(step, bufs, ss, rs, cut):
        out = []
        for part in range(2):
            for up in (True, False):
                out.append(plane(bufs[part], part == 0, step, up, ss.at[part], rs.at[part], cut))
        return out

    def own_rows():
        @pl.when(x >= 2)
        def _():
            c1.wait_recv()

        def put(src):
            a = pltpu.make_async_copy(src.at[pl.ds(0, 32)], ra.at[y, x], lsem.at[6])
            b = pltpu.make_async_copy(src.at[pl.ds(32, 32)], rb.at[x, y], lsem.at[7])
            a.start()
            b.start()
            a.wait()
            b.wait()

        @pl.when(x >= 2)
        def _():
            put(rhalf)

        @pl.when(x < 2)
        def _():
            put(rows_b)

    for step in range(1, 5):
        cs = plane_step(step, (ga, gb), sp, rp, cut_lead)
        for s, _ in cs:
            s.start()
        if step == 1:
            own_rows()
        for _, r in cs:
            r.wait_recv()

    def strip_start(step):
        for s, _ in plane_step(step, (ra, rb), sq, rq, cut_strip):
            s.start()

    def strip_recv(step):
        for _, r in plane_step(step, (ra, rb), sq, rq, cut_strip):
            r.wait_recv()

    def ring_start(step):
        for c in ring(step):
            c.start()

    def progress(J):
        @pl.when(J == 1)
        def _():
            strip_recv(1)
            strip_start(2)
            ring_recv(1)
            ring_start(2)

        @pl.when(J == 2)
        def _():
            strip_recv(2)
            strip_start(3)

        @pl.when(J == 3)
        def _():
            ring_recv(2)
            ring_start(3)

        @pl.when(J == 5)
        def _():
            strip_recv(3)
            strip_start(4)
            ring_recv(3)
            ring_start(4)

    strip_start(1)
    lead_body(ga, gb, u_ref, w_ref, progress)
    strip_recv(4)
    ring_recv(4)

    for step in range(1, 5):
        for s, _ in plane_step(step, (ga, gb), sp, rp, cut_lead) + plane_step(step, (ra, rb), sq, rq, cut_strip):
            s.wait_send()
        for c in ring(step):
            c.wait_send()

    @pl.when(x < 2)
    def _():
        c0.wait_send()
        c1.wait_send()

    @pl.when(mine < ND)
    def _():
        for d in range(1, NZ):
            zsend(0, d).wait_send()
            zsend(1, d).wait_send()


def factor_block(block):
    sub = lax.broadcasted_iota(jnp.int32, (8, T), 0)
    lane = lax.broadcasted_iota(jnp.int32, (8, T), 1)
    V = [block[8 * s : 8 * s + 8, :] for s in range(16)]
    W = [jnp.where(lane == sub + 8 * s, 1.0, 0.0).astype(F32) for s in range(16)]
    lb = lambda v, j: jnp.broadcast_to(v[:, j : j + 1], (8, T))
    sb = lambda v, k: jnp.broadcast_to(v[k : k + 1, :], (8, T))
    for t in range(16):
        v, w = V[t], W[t]
        C = [lb(v, 8 * t + j) for j in range(8)]
        rv, rw, rs, uk = [], [], [], []
        for k in range(8):
            r = lax.rsqrt(sb(C[k], k))
            a, b = sb(v, k) * r, sb(w, k) * r
            m = jnp.where(sub > k, C[k] * r, 0.0)
            us = {}
            for j in range(k + 1, 8):
                us[j] = sb(C[j], k) * r
                C[j] = C[j] - m * us[j]
            v = jnp.where(sub == k, a, v - m * a)
            w = jnp.where(sub == k, b, w - m * b)
            rv.append(a)
            rw.append(b)
            rs.append(r)
            uk.append(us)
        V[t], W[t] = v, w
        for s in range(t + 1, 16):
            Cs = [lb(V[s], 8 * t + j) for j in range(8)]
            vs, ws = V[s], W[s]
            for k in range(8):
                m = Cs[k] * rs[k]
                for j in range(k + 1, 8):
                    Cs[j] = Cs[j] - m * uk[k][j]
                vs = vs - m * rv[k]
                ws = ws - m * rw[k]
            V[s], W[s] = vs, ws
    return jnp.concatenate(W, axis=0)


def lead_body(ga, gb, u_ref, w_ref, progress):
    for i in range(NB):
        y = i % 4
        top, bot = (0, 3) if i < 4 else (1, 2)
        for d in range(ND):
            j = (i + d) % NB
            if d == 4 and i >= 4:
                continue
            parts = [ga[y, top, d], gb[top, y, d], ga[y, bot, d], gb[bot, y, d]]
            if j >= i:
                for k in range(4):
                    u_ref[i * T + 32 * k : i * T + 32 * k + 32, j * T : j * T + T] = parts[k]
            else:
                u_ref[j * T : j * T + T, i * T : i * T + T] = jnp.concatenate(parts, axis=0).T
    for i in range(1, NB):
        u_ref[i * T : i * T + T, 0 : i * T] = jnp.zeros((T, i * T), F32)
    col = lax.broadcasted_iota(jnp.int32, (T, LEAD), 1)
    sub = lax.broadcasted_iota(jnp.int32, (T, LEAD), 0)

    def body(J, _):
        progress(J)
        j0 = pl.multiple_of(J * T, T)
        inv = factor_block(u_ref[pl.ds(j0, T), pl.ds(j0, T)])
        w_ref[J] = inv
        U = dot3(inv, u_ref[pl.ds(j0, T), :], NN)
        u_ref[pl.ds(j0, T), :] = jnp.where(col >= sub + j0, U, 0.0)

        def upd(I, _):
            i0 = pl.multiple_of(I * T, T)
            ui = u_ref[pl.ds(j0, T), pl.ds(i0, T)]
            u_ref[pl.ds(i0, T), :] = u_ref[pl.ds(i0, T), :] - dot3(ui, u_ref[pl.ds(j0, T), :], TN)
            return 0

        lax.fori_loop(J + 1, NB, upd, 0)
        return 0

    lax.fori_loop(0, NB, body, 0)


def panels(front):
    vm = pl.BlockSpec(memory_space=pltpu.VMEM)
    dma = pltpu.SemaphoreType.DMA
    return pl.pallas_call(
        panel_kernel,
        out_shape=(
            jax.ShapeDtypeStruct((LEAD, LEAD), F32),
            jax.ShapeDtypeStruct((NB, T, T), F32),
            jax.ShapeDtypeStruct((4, 4, 32, COLS), BF16),
            jax.ShapeDtypeStruct((4, 4, 32, COLS), BF16),
            jax.ShapeDtypeStruct((NZ, ROWS, T), F32),
        ),
        in_specs=[pl.BlockSpec(memory_space=pl.ANY)],
        out_specs=(vm,) * 5,
        scratch_shapes=[
            pltpu.VMEM((4, 4, ND, 32, T), F32), pltpu.VMEM((4, 4, ND, 32, T), F32),
            pltpu.VMEM((T, COLS), F32), pltpu.VMEM((T, COLS), BF16), pltpu.VMEM((T, T), F32),
            pltpu.VMEM((64, T), F32), pltpu.VMEM((64, COLS), BF16),
            dma((8,)), dma((2,)), dma((2,)), dma((2, NZ)), dma((2, ND)),
            dma((2, 4, 2)), dma((2, 4, 2)), dma((2, 4, 2)), dma((2, 4, 2)), dma((2, 4)), dma((2, 4)),
        ],
        compiler_params=pltpu.CompilerParams(collective_id=0, has_side_effects=True, vmem_limit_bytes=VMEM_LIMIT),
        name="panels",
    )(front)


def one_hot(rm_ref, team, first, start, out):
    sub = lax.broadcasted_iota(jnp.int32, (ROWS, T), 0)
    for s in range(RT):
        tile = s * 16 + first
        line = rm_ref[team, pl.ds(jnp.maximum(tile - NB, 0), 1), :]
        spot = jnp.where(tile >= NB, (line // 2048) * T + line % T, -1)
        out[:, s * T : s * T + T] = jnp.where(sub == spot, 1.0, 0.0).astype(BF16)


def update_kernel(front, ra, rb, zs, u_ref, w_ref, rm_ref, fac, placed, ub, xb, yb, upd, pr, pe, po):
    team = lax.axis_index("team")
    pos = lax.axis_index("row")
    z = lax.axis_index("col")
    ub[...] = u_ref[...].astype(BF16)
    one_hot(rm_ref, team, pos, 0, pr)
    one_hot(rm_ref, team, z, 0, pe)
    one_hot(rm_ref, team, z + NZ, 0, po)
    r = lax.broadcasted_iota(jnp.int32, (T, T), 0)
    c = lax.broadcasted_iota(jnp.int32, (T, T), 1)
    for J in range(NB):
        cs = slice(J * T, J * T + T)
        acc = zs[J]
        if J:
            acc = acc - dot1(xb[:, : J * T], ub[: J * T, cs], NN)
        xj = dot3(acc, w_ref[J], NT)
        xb[:, cs] = xj.astype(BF16)
        fac[T:, cs] = xj[T:]
        fac[:T, cs] = jnp.where(pos * T + r >= J * T + c, xj[:T], 0.0)

    wide = 512

    def ystep(n, _):
        n0 = pl.multiple_of(n * wide, wide)
        for J in range(NB):
            cs = slice(J * T, J * T + T)
            y = J % 4
            top, bot = (0, 3) if J < 4 else (1, 2)
            parts = [ra[y, top, :, pl.ds(n0, wide)], rb[top, y, :, pl.ds(n0, wide)], ra[y, bot, :, pl.ds(n0, wide)], rb[bot, y, :, pl.ds(n0, wide)]]
            acc = jnp.concatenate(parts, axis=0).astype(F32)
            if J:
                acc = acc - dot1(ub[: J * T, cs], yb[: J * T, pl.ds(n0, wide)], TN)
            yj = dot3(w_ref[J], acc, NN)
            yb[cs, pl.ds(n0, wide)] = yj.astype(BF16)
        return 0

    lax.fori_loop(0, COLS // wide, ystep, 0)

    def ustep(n, _):
        n0 = pl.multiple_of(n * 256, 256)
        upd[:, pl.ds(n0, 256)] = (front[0, :, pl.ds(n0, 256)] - dot1(xb[...], yb[:, pl.ds(n0, 256)], NN)).astype(BF16)
        t = dot1(pr[...], upd[:, pl.ds(n0, 256)], NN).astype(BF16)
        upd[:, pl.ds(n0, 256)] = t
        return 0

    lax.fori_loop(0, COLS // 256, ustep, 0)
    even = jnp.concatenate([upd[:, 2 * s * T : 2 * s * T + T] for s in range(RT)], axis=1)
    odd = jnp.concatenate([upd[:, (2 * s + 1) * T : (2 * s + 2) * T] for s in range(RT)], axis=1)
    for s in range(RT):
        placed[:, 2 * s * T : 2 * s * T + T] = dot1(even, pe[s * T : s * T + T, :], NT).astype(BF16)
        placed[:, (2 * s + 1) * T : (2 * s + 2) * T] = dot1(odd, po[s * T : s * T + T, :], NT).astype(BF16)


def update(front, ra, rb, zs, u, w, rm):
    vm = pl.BlockSpec(memory_space=pltpu.VMEM)
    return pl.pallas_call(
        update_kernel,
        out_shape=(jax.ShapeDtypeStruct((ROWS, LEAD), F32), jax.ShapeDtypeStruct((ROWS, COLS), BF16)),
        in_specs=[vm] * 7,
        out_specs=(vm, vm),
        scratch_shapes=[
            pltpu.VMEM((LEAD, LEAD), BF16), pltpu.VMEM((ROWS, LEAD), BF16), pltpu.VMEM((LEAD, COLS), BF16),
            pltpu.VMEM((ROWS, COLS), BF16), pltpu.VMEM((ROWS, ROWS), BF16), pltpu.VMEM((ROWS, ROWS), BF16), pltpu.VMEM((ROWS, ROWS), BF16),
        ],
        compiler_params=pltpu.CompilerParams(vmem_limit_bytes=VMEM_LIMIT),
        name="update",
    )(front, ra, rb, zs, u, w, rm)


def shards(front, row_map, tile_owner):
    team = lax.axis_index("team")
    pos = lax.axis_index("row")
    u, w, ra, rb, zs = panels(front)
    fac, placed = update(front, ra, rb, zs, u, w, row_map.reshape(2, -1, T))
    other = lax.ppermute(placed, "team", [(0, 1), (1, 0)])
    owned = jnp.take(tile_owner, jnp.arange(RT) * 16 + pos) == team
    owned = jnp.repeat(owned, T)
    assembled = jnp.where(owned[:, None], placed.astype(F32) + other.astype(F32), 0.0)
    return fac[None], assembled[None]


def solution(mesh):
    return jax.shard_map(
        shards,
        mesh=mesh,
        in_specs=(P("team", "row", "col"), P(), P()),
        out_specs=(P("team", "row", None), P("team", "row", "col")),
        check_vma=False,
    )
```

```python
import jax
import jax.numpy as jnp
from jax import lax
from jax.experimental import pallas as pl
from jax.experimental.pallas import tpu as pltpu
from jax.sharding import PartitionSpec as P

T = 128
LEAD = 1024
NB = 8
RT = 6
CT = 12
ROWS = RT * T
COLS = CT * T
NZ = 8
ND = 5
MESH = pl.DeviceIdType.MESH
VMEM_LIMIT = 60 << 20
F32 = jnp.float32
BF16 = jnp.bfloat16
NN = (((1,), (0,)), ((), ()))
NT = (((1,), (1,)), ((), ()))
TN = (((0,), (0,)), ((), ()))


def dot1(a, b, dims):
    return lax.dot_general(a, b, dims, preferred_element_type=F32)


def split(a):
    hi = a.astype(BF16)
    return hi, (a - hi.astype(F32)).astype(BF16)


def dot3(a, b, dims):
    ah, al = split(a)
    bh, bl = split(b)
    return dot1(ah, bh, dims) + dot1(ah, bl, dims) + dot1(al, bh, dims)


def row_of(x, y):
    return y + jnp.where((x == 0) | (x == 3), 0, 4)


def panel_kernel(front, rm_ref, x_out, own_out, other_out,
                 ab, ra, rb, zs, u_ref, ub, w_ref, xb, yb, upd, tmp, pr, pc, placed,
                 ga, gb, rows_f, rows_b, tile, half, rhalf,
                 lsem, s0, r0, sz, rz, sp, rp, sq, rq, sr, rr, st, rt, lt):
    team = lax.axis_index("team")
    pos = lax.axis_index("row")
    z = lax.axis_index("col")
    x, y = pos // 4, pos % 4
    xs = lambda d: ((x + d) % 4) * 4 + y
    ys = lambda d: x * 4 + (y + d) % 4
    row = row_of(x, y)

    c_col = pltpu.make_async_copy(front.at[0, :, pl.ds(0, T)], zs.at[z], lsem.at[0])
    c_row = pltpu.make_async_copy(front.at[0, pl.ds(0, T), :], rows_f, lsem.at[1])
    c_tile = pltpu.make_async_copy(front.at[0, pl.ds(0, T), pl.ds(0, T)], tile, lsem.at[2])
    c_half = pltpu.make_async_copy(front.at[0, pl.ds(0, 64), pl.ds(0, T)], half, lsem.at[3])
    c_tile.start()
    c_row.start()
    c_col.start()
    c_block = pltpu.make_async_copy(front.at[0], ab, lsem.at[8])
    c_out = pltpu.make_async_copy(xb, x_out, lsem.at[9])

    @pl.when(x < 2)
    def _():
        c_half.start()

    bar = pltpu.get_barrier_semaphore()
    for d in (1, 3):
        pl.semaphore_signal(bar, inc=1, device_id={"row": xs(d)}, device_id_type=MESH)
        pl.semaphore_signal(bar, inc=1, device_id={"row": ys(d)}, device_id_type=MESH)
    for d in range(1, NZ):
        pl.semaphore_signal(bar, inc=1, device_id={"col": (z + d) % NZ}, device_id_type=MESH)
    pl.semaphore_signal(bar, inc=1, device_id={"team": 1 - team}, device_id_type=MESH)
    for ref in (ub, xb, yb):
        ref[...] = jnp.zeros_like(ref)
    c_row.wait()
    rows_b[...] = rows_f[...].astype(BF16)
    c_tile.wait()
    c_col.wait()

    @pl.when(x < 2)
    def _():
        c_half.wait()

    pl.semaphore_wait(bar, 4 + NZ)

    mirror = {"row": (3 - x) * 4 + y}
    c0 = pltpu.make_async_remote_copy(tile.at[pl.ds(64, 64)], half, s0.at[0], r0.at[0], device_id=mirror, device_id_type=MESH)
    c1 = pltpu.make_async_remote_copy(rows_b.at[pl.ds(64, 64)], rhalf, s0.at[1], r0.at[1], device_id=mirror, device_id_type=MESH)

    @pl.when(x < 2)
    def _():
        c0.start()
        c1.start()

    def ring(step):
        up, dn = (z - step + 1 + NZ) % NZ, (z + step - 1) % NZ
        if step < 4:
            src_u, src_d = zs.at[up], zs.at[dn]
        else:
            src_u, src_d = zs.at[up, pl.ds(0, ROWS // 2)], zs.at[dn, pl.ds(ROWS // 2, ROWS // 2)]
        a = pltpu.make_async_remote_copy(src_u, src_u, sr.at[0, step - 1], rr.at[0, step - 1], device_id={"col": (z + 1) % NZ}, device_id_type=MESH)
        b = pltpu.make_async_remote_copy(src_d, src_d, sr.at[1, step - 1], rr.at[1, step - 1], device_id={"col": (z + NZ - 1) % NZ}, device_id_type=MESH)
        return a, b

    def ring_recv(step):
        up, dn = (z - step + NZ) % NZ, (z + step) % NZ
        if step < 4:
            dst_u, dst_d = zs.at[up], zs.at[dn]
        else:
            dst_u, dst_d = zs.at[up, pl.ds(0, ROWS // 2)], zs.at[dn, pl.ds(ROWS // 2, ROWS // 2)]
        pltpu.make_async_remote_copy(dst_u, dst_u, sr.at[0, step - 1], rr.at[0, step - 1], device_id={"col": (z + 1) % NZ}, device_id_type=MESH).wait_recv()
        pltpu.make_async_remote_copy(dst_d, dst_d, sr.at[1, step - 1], rr.at[1, step - 1], device_id={"col": (z + NZ - 1) % NZ}, device_id_type=MESH).wait_recv()

    @pl.when(x >= 2)
    def _():
        c0.wait_recv()

    mine = (z - row + NZ) % NZ
    o1 = pltpu.make_async_copy(half.at[pl.ds(0, 32)], ga.at[y, x, jnp.minimum(mine, ND - 1)], lsem.at[4])
    o2 = pltpu.make_async_copy(half.at[pl.ds(32, 32)], gb.at[x, y, jnp.minimum(mine, ND - 1)], lsem.at[5])

    def zsend(k, d):
        slot = jnp.minimum(mine, ND - 1)
        dst = ga.at[y, x, slot] if k == 0 else gb.at[x, y, slot]
        return pltpu.make_async_remote_copy(half.at[pl.ds(32 * k, 32)], dst, sz.at[k, d], rz.at[k, slot], device_id={"col": (z + d) % NZ}, device_id_type=MESH)

    @pl.when(mine < ND)
    def _():
        for d in (4, 3, 5, 2, 6, 1, 7):
            zsend(0, d).start()
            zsend(1, d).start()
        o1.start()
        o2.start()
        o1.wait()
        o2.wait()

    for d in range(ND):
        @pl.when(mine != d)
        def _():
            pltpu.make_async_remote_copy(half.at[pl.ds(0, 32)], ga.at[y, x, d], sz.at[0, 0], rz.at[0, d], device_id={"col": (z + 1) % NZ}, device_id_type=MESH).wait_recv()
            pltpu.make_async_remote_copy(half.at[pl.ds(32, 32)], gb.at[x, y, d], sz.at[1, 0], rz.at[1, d], device_id={"col": (z + 1) % NZ}, device_id_type=MESH).wait_recv()

    for c in ring(1):
        c.start()
    c_block.start()

    def plane(buf, first, step, up, ss, rs, cut):
        f, s = (x, y) if first else (y, x)
        fd, sd = (xs, ys) if first else (ys, xs)
        if step <= 2:
            base = lambda d: buf.at[s, (f + d) % 4]
            dev = fd
        else:
            base = lambda d: buf.at[(s + d) % 4]
            dev = sd
        me = step - 1
        if step % 2 == 1:
            src, rcv = base(0), base(3 if up else 1)
        else:
            src, rcv = base(3 if up else 1), base(2)
            src, rcv = cut(src, up, step), cut(rcv, up, step)
        k = 0 if up else 1
        to = {"row": dev(1 if up else 3)}
        send = pltpu.make_async_remote_copy(src, src, ss.at[me, k], rs.at[me, k], device_id=to, device_id_type=MESH)
        recv = pltpu.make_async_remote_copy(rcv, rcv, ss.at[me, k], rs.at[me, k], device_id=to, device_id_type=MESH)
        return send, recv

    def cut_lead(ref, up, step):
        h = pl.ds(0 if up else 16, 16)
        return ref.at[:, h] if step == 2 else ref.at[:, :, h]

    def cut_strip(ref, up, step):
        h = pl.ds(0 if up else 16, 16)
        return ref.at[h] if step == 2 else ref.at[:, h]

    def plane_step(step, bufs, ss, rs, cut):
        out = []
        for part in range(2):
            for up in (True, False):
                out.append(plane(bufs[part], part == 0, step, up, ss.at[part], rs.at[part], cut))
        return out

    def own_rows():
        @pl.when(x >= 2)
        def _():
            c1.wait_recv()

        def put(src):
            a = pltpu.make_async_copy(src.at[pl.ds(0, 32)], ra.at[y, x], lsem.at[6])
            b = pltpu.make_async_copy(src.at[pl.ds(32, 32)], rb.at[x, y], lsem.at[7])
            a.start()
            b.start()
            a.wait()
            b.wait()

        @pl.when(x >= 2)
        def _():
            put(rhalf)

        @pl.when(x < 2)
        def _():
            put(rows_b)

    for step in range(1, 5):
        cs = plane_step(step, (ga, gb), sp, rp, cut_lead)
        for s, _ in cs:
            s.start()
        if step == 1:
            own_rows()
            one_hot(rm_ref, team, z, pc.at[0])
        elif step == 3:
            one_hot(rm_ref, team, z + NZ, pc.at[1])
            one_hot(rm_ref, team, pos, pr)
        for _, r in cs:
            r.wait_recv()

    def strip_start(step):
        for s, _ in plane_step(step, (ra, rb), sq, rq, cut_strip):
            s.start()

    def strip_recv(step):
        for _, r in plane_step(step, (ra, rb), sq, rq, cut_strip):
            r.wait_recv()

    def ring_start(step):
        for c in ring(step):
            c.start()

    def progress(J):
        @pl.when(J == 0)
        def _():
            ring_recv(1)
            ring_start(2)

        @pl.when(J == 1)
        def _():
            strip_recv(1)
            strip_start(2)

        @pl.when(J == 2)
        def _():
            strip_recv(2)
            strip_start(3)
            ring_recv(2)
            ring_start(3)

        @pl.when(J == 4)
        def _():
            strip_recv(3)
            strip_start(4)
            ring_recv(3)
            ring_start(4)

    strip_start(1)
    assemble(ga, gb, u_ref)

    def ready():
        strip_recv(4)
        ring_recv(4)

    def tile_copies(slot):
        cs = pl.ds(slot * T, T)
        far = pltpu.make_async_remote_copy(placed.at[:, cs], other_out.at[:, cs], st.at[slot], rt.at[slot], device_id={"team": 1 - team}, device_id_type=MESH)
        near = pltpu.make_async_copy(placed.at[:, cs], own_out.at[:, cs], lt.at[slot])
        return far, near

    pending = []

    def flush():
        for slot in pending:
            for c in tile_copies(slot):
                c.start()
        pending.clear()

    def send(c, n):
        flush()
        pending.extend(2 * (2 * n + h) + c for h in range(2))

    core(pos, ab, ra, rb, zs, u_ref, ub, w_ref, xb, yb, upd, tmp, pr, pc, placed,
         progress, ready, c_block.wait, c_out.start, send)
    flush()

    for step in range(1, 5):
        for s, _ in plane_step(step, (ga, gb), sp, rp, cut_lead) + plane_step(step, (ra, rb), sq, rq, cut_strip):
            s.wait_send()
        for c in ring(step):
            c.wait_send()

    for slot in range(CT):
        far, near = tile_copies(slot)
        far.wait()
        near.wait()
    c_out.wait()

    @pl.when(x < 2)
    def _():
        c0.wait_send()
        c1.wait_send()

    @pl.when(mine < ND)
    def _():
        for d in range(1, NZ):
            zsend(0, d).wait_send()
            zsend(1, d).wait_send()


def factor_block(block):
    sub = lax.broadcasted_iota(jnp.int32, (8, T), 0)
    lane = lax.broadcasted_iota(jnp.int32, (8, T), 1)
    V = [block[8 * s : 8 * s + 8, :] for s in range(16)]
    W = [jnp.where(lane == sub + 8 * s, 1.0, 0.0).astype(F32) for s in range(16)]
    lb = lambda v, j: jnp.broadcast_to(v[:, j : j + 1], (8, T))
    sb = lambda v, k: jnp.broadcast_to(v[k : k + 1, :], (8, T))
    for t in range(16):
        v, w = V[t], W[t]
        C = [lb(v, 8 * t + j) for j in range(8)]
        rv, rw, rs, uk = [], [], [], []
        for k in range(8):
            r = lax.rsqrt(sb(C[k], k))
            a, b = sb(v, k) * r, sb(w, k) * r
            m = jnp.where(sub > k, C[k] * r, 0.0)
            us = {}
            for j in range(k + 1, 8):
                us[j] = sb(C[j], k) * r
                C[j] = C[j] - m * us[j]
            v = jnp.where(sub == k, a, v - m * a)
            w = jnp.where(sub == k, b, w - m * b)
            rv.append(a)
            rw.append(b)
            rs.append(r)
            uk.append(us)
        V[t], W[t] = v, w
        for s in range(t + 1, 16):
            Cs = [lb(V[s], 8 * t + j) for j in range(8)]
            vs, ws = V[s], W[s]
            for k in range(8):
                m = Cs[k] * rs[k]
                for j in range(k + 1, 8):
                    Cs[j] = Cs[j] - m * uk[k][j]
                vs = vs - m * rv[k]
                ws = ws - m * rw[k]
            V[s], W[s] = vs, ws
    return jnp.concatenate(W, axis=0)


def assemble(ga, gb, u_ref):
    for i in range(NB):
        y = i % 4
        top, bot = (0, 3) if i < 4 else (1, 2)
        for d in range(ND):
            j = (i + d) % NB
            if d == 4 and i >= 4:
                continue
            parts = [ga[y, top, d], gb[top, y, d], ga[y, bot, d], gb[bot, y, d]]
            if j >= i:
                for k in range(4):
                    u_ref[i * T + 32 * k : i * T + 32 * k + 32, j * T : j * T + T] = parts[k]
            else:
                u_ref[j * T : j * T + T, i * T : i * T + T] = jnp.concatenate(parts, axis=0).T
    for i in range(1, NB):
        u_ref[i * T : i * T + T, 0 : i * T] = jnp.zeros((T, i * T), F32)


def lead_step(J, u_ref, ub, w_ref, filler):
    col = lax.broadcasted_iota(jnp.int32, (T, LEAD), 1)
    sub = lax.broadcasted_iota(jnp.int32, (T, LEAD), 0)
    j0 = pl.multiple_of(J * T, T)
    filler()
    inv = factor_block(u_ref[pl.ds(j0, T), pl.ds(j0, T)])
    w_ref[J] = inv
    U = jnp.where(col >= sub + j0, dot3(inv, u_ref[pl.ds(j0, T), :], NN), 0.0)
    u_ref[pl.ds(j0, T), :] = U
    ub[pl.ds(j0, T), :] = U.astype(BF16)

    def upd(I, _):
        i0 = pl.multiple_of(I * T, T)
        ui = u_ref[pl.ds(j0, T), pl.ds(i0, T)]
        u_ref[pl.ds(i0, T), :] = u_ref[pl.ds(i0, T), :] - dot3(ui, u_ref[pl.ds(j0, T), :], TN)
        return 0

    lax.fori_loop(J + 1, NB, upd, 0)


def one_hot(rm_ref, team, first, out):
    sub = lax.broadcasted_iota(jnp.int32, (ROWS, T), 0)
    for s in range(RT):
        tile = s * 16 + first
        line = rm_ref[team, pl.ds(jnp.maximum(tile - NB, 0), 1), :]
        spot = jnp.where(tile >= NB, (line // 2048) * T + line % T, -1)
        out[:, s * T : s * T + T] = jnp.where(sub == spot, 1.0, 0.0).astype(BF16)


def solve(J, depth, pos, ra, rb, zs, ub, w_ref, xb, yb):
    j0 = pl.multiple_of(J * T, T)
    cs = pl.ds(j0, T)
    acc = zs[J]
    if depth:
        acc = acc - dot1(xb[:, :depth], ub[:depth, cs], NN)
    xj = dot3(acc, w_ref[J], NT)
    r = lax.broadcasted_iota(jnp.int32, (T, T), 0)
    c = lax.broadcasted_iota(jnp.int32, (T, T), 1)
    xb[T:, cs] = xj[T:].astype(BF16)
    xb[:T, cs] = jnp.where(pos * T + r >= j0 + c, xj[:T], 0.0).astype(BF16)
    y, top = J % 4, J // 4
    acc = jnp.concatenate([ra[y, top], rb[top, y], ra[y, 3 - top], rb[3 - top, y]], axis=0).astype(F32)
    if depth:
        acc = acc - dot1(ub[:depth, cs], yb[:depth, :], TN)
    yb[cs, :] = dot3(w_ref[J], acc, NN).astype(BF16)


def place(pr, pc, upd, tmp, placed, send):
    for c in range(2):
        for n in range(3):
            cs = slice(n * 256, n * 256 + 256)
            tmp[c, :, cs] = dot1(pr[...], upd[c, :, cs], NN).astype(BF16)
        for n in range(3):
            out = dot1(tmp[c], pc[c, n * 256 : n * 256 + 256, :], NT).astype(BF16)
            for h in range(2):
                slot = 2 * (2 * n + h) + c
                placed[:, slot * T : slot * T + T] = out[:, h * T : h * T + T]
            send(c, n)


def core(pos, ab, ra, rb, zs, u_ref, ub, w_ref, xb, yb, upd, tmp, pr, pc, placed, progress, ready, block_ready, solved, send):
    nothing = lambda: None

    def early(J, _):
        progress(J)
        lead_step(J, u_ref, ub, w_ref, nothing)
        return 0

    lax.fori_loop(0, 5, early, 0)
    ready()
    args = (pos, ra, rb, zs, ub, w_ref, xb, yb)

    def late(J, _):
        def filler():
            for k in range(3):
                solve(3 * (J - 5) + k, LEAD, *args)

        lead_step(J, u_ref, ub, w_ref, filler)
        return 0

    lax.fori_loop(5, 7, late, 0)
    block_ready()

    def last():
        for n in range(6):
            cs = slice(n * 256, n * 256 + 256)
            ab[:, cs] = ab[:, cs] - dot1(xb[:, : 6 * T], yb[: 6 * T, cs], NN)
        solve(6, 6 * T, *args)

    lead_step(7, u_ref, ub, w_ref, last)
    solve(7, 7 * T, *args)
    solved()
    for n in range(6):
        cs = slice(n * 256, n * 256 + 256)
        v = (ab[:, cs] - dot1(xb[:, 6 * T :], yb[6 * T :, cs], NN)).astype(BF16)
        upd[0, :, n * T : n * T + T] = v[:, :T]
        upd[1, :, n * T : n * T + T] = v[:, T:]
    place(pr, pc, upd, tmp, placed, send)


def panels(front, rm):
    vm = pl.BlockSpec(memory_space=pltpu.VMEM)
    hbm = pl.BlockSpec(memory_space=pl.ANY)
    dma = pltpu.SemaphoreType.DMA
    v = pltpu.VMEM
    return pl.pallas_call(
        panel_kernel,
        out_shape=(
            jax.ShapeDtypeStruct((ROWS, LEAD), BF16),
            jax.ShapeDtypeStruct((ROWS, COLS), BF16),
            jax.ShapeDtypeStruct((ROWS, COLS), BF16),
        ),
        in_specs=[hbm, vm],
        out_specs=(hbm,) * 3,
        scratch_shapes=[
            v((ROWS, COLS), F32), v((4, 4, 32, COLS), BF16), v((4, 4, 32, COLS), BF16), v((NZ, ROWS, T), F32),
            v((LEAD, LEAD), F32), v((LEAD, LEAD), BF16), v((NB, T, T), F32), v((ROWS, LEAD), BF16), v((LEAD, COLS), BF16),
            v((2, ROWS, ROWS), BF16), v((2, ROWS, ROWS), BF16), v((ROWS, ROWS), BF16), v((2, ROWS, ROWS), BF16), v((ROWS, COLS), BF16),
            v((4, 4, ND, 32, T), F32), v((4, 4, ND, 32, T), F32),
            v((T, COLS), F32), v((T, COLS), BF16), v((T, T), F32), v((64, T), F32), v((64, COLS), BF16),
            dma((10,)), dma((2,)), dma((2,)), dma((2, NZ)), dma((2, ND)),
            dma((2, 4, 2)), dma((2, 4, 2)), dma((2, 4, 2)), dma((2, 4, 2)), dma((2, 4)), dma((2, 4)),
            dma((CT,)), dma((CT,)), dma((CT,)),
        ],
        compiler_params=pltpu.CompilerParams(collective_id=0, has_side_effects=True, vmem_limit_bytes=VMEM_LIMIT),
        name="panels",
    )(front, rm)


def shards(front, row_map, tile_owner):
    team = lax.axis_index("team")
    pos = lax.axis_index("row")
    xb, own, other = panels(front, row_map.reshape(2, -1, T))
    owned = jnp.take(tile_owner, jnp.arange(RT) * 16 + pos) == team
    owned = jnp.repeat(owned, T)
    assembled = jnp.where(owned[:, None], own.astype(F32) + other.astype(F32), 0.0)
    return xb.astype(F32)[None], assembled[None]


def solution(mesh):
    return jax.shard_map(
        shards,
        mesh=mesh,
        in_specs=(P("team", "row", "col"), P(), P()),
        out_specs=(P("team", "row", None), P("team", "row", "col")),
        check_vma=False,
    )
```

```python
import jax
import jax.numpy as jnp
from jax import lax
from jax.experimental import pallas as pl
from jax.experimental.pallas import tpu as pltpu
from jax.sharding import PartitionSpec as P

T = 128
LEAD = 1024
NB = 8
RT = 6
CT = 12
ROWS = RT * T
COLS = CT * T
NZ = 8
ND = 5
MESH = pl.DeviceIdType.MESH
VMEM_LIMIT = 60 << 20
F32 = jnp.float32
BF16 = jnp.bfloat16
NN = (((1,), (0,)), ((), ()))
NT = (((1,), (1,)), ((), ()))
TN = (((0,), (0,)), ((), ()))


def dot1(a, b, dims):
    return lax.dot_general(a, b, dims, preferred_element_type=F32)


def split(a):
    hi = a.astype(BF16)
    return hi, (a - hi.astype(F32)).astype(BF16)


def dot3(a, b, dims):
    ah, al = split(a)
    bh, bl = split(b)
    return dot1(ah, bh, dims) + dot1(ah, bl, dims) + dot1(al, bh, dims)


def row_of(x, y):
    return y + jnp.where((x == 0) | (x == 3), 0, 4)


def panel_kernel(front, rm_ref, x_out, own_out, other_out,
                 ab, ra, rb, zs, u_ref, ub, ul, w_ref, dref, rbuf, wprev, xb, yb, upd, tmp, pr, pc, placed,
                 ga, gb, rows_f, rows_b, tile, rhalf,
                 lsem, s0, r0, sz, rz, sp, rp, sq, rq, sr, rr, st, rt, lt):
    team = lax.axis_index("team")
    pos = lax.axis_index("row")
    z = lax.axis_index("col")
    x, y = pos // 4, pos % 4
    xs = lambda d: ((x + d) % 4) * 4 + y
    ys = lambda d: x * 4 + (y + d) % 4
    row = row_of(x, y)

    c_col = pltpu.make_async_copy(front.at[0, :, pl.ds(0, T)], zs.at[z], lsem.at[0])
    c_row = pltpu.make_async_copy(front.at[0, pl.ds(0, T), :], rows_f, lsem.at[1])
    c_tile = pltpu.make_async_copy(front.at[0, pl.ds(0, T), pl.ds(0, T)], tile, lsem.at[2])
    c_tile.start()
    c_row.start()
    c_col.start()
    c_block = pltpu.make_async_copy(front.at[0], ab, lsem.at[8])
    c_out = pltpu.make_async_copy(xb, x_out, lsem.at[9])

    bar = pltpu.get_barrier_semaphore()
    for d in (1, 3):
        pl.semaphore_signal(bar, inc=1, device_id={"row": xs(d)}, device_id_type=MESH)
        pl.semaphore_signal(bar, inc=1, device_id={"row": ys(d)}, device_id_type=MESH)
    for d in range(1, NZ):
        pl.semaphore_signal(bar, inc=1, device_id={"col": (z + d) % NZ}, device_id_type=MESH)
    pl.semaphore_signal(bar, inc=1, device_id={"team": 1 - team}, device_id_type=MESH)
    for ref in (ub, ul, rbuf, wprev, xb, yb):
        ref[...] = jnp.zeros_like(ref)
    for d in range(1, NZ):
        pl.semaphore_signal(bar, inc=1, device_id={"row": (3 - x) * 4 + y, "col": (z + d) % NZ}, device_id_type=MESH)
    c_tile.wait()
    pl.semaphore_wait(bar, 4 + NZ + NZ - 1)

    mirror = {"row": (3 - x) * 4 + y}
    c1 = pltpu.make_async_remote_copy(rows_b.at[pl.ds(64, 64)], rhalf, s0.at[1], r0.at[1], device_id=mirror, device_id_type=MESH)

    def ring(step):
        up, dn = (z - step + 1 + NZ) % NZ, (z + step - 1) % NZ
        if step < 4:
            src_u, src_d = zs.at[up], zs.at[dn]
        else:
            src_u, src_d = zs.at[up, pl.ds(0, ROWS // 2)], zs.at[dn, pl.ds(ROWS // 2, ROWS // 2)]
        a = pltpu.make_async_remote_copy(src_u, src_u, sr.at[0, step - 1], rr.at[0, step - 1], device_id={"col": (z + 1) % NZ}, device_id_type=MESH)
        b = pltpu.make_async_remote_copy(src_d, src_d, sr.at[1, step - 1], rr.at[1, step - 1], device_id={"col": (z + NZ - 1) % NZ}, device_id_type=MESH)
        return a, b

    def ring_recv(step):
        up, dn = (z - step + NZ) % NZ, (z + step) % NZ
        if step < 4:
            dst_u, dst_d = zs.at[up], zs.at[dn]
        else:
            dst_u, dst_d = zs.at[up, pl.ds(0, ROWS // 2)], zs.at[dn, pl.ds(ROWS // 2, ROWS // 2)]
        pltpu.make_async_remote_copy(dst_u, dst_u, sr.at[0, step - 1], rr.at[0, step - 1], device_id={"col": (z + 1) % NZ}, device_id_type=MESH).wait_recv()
        pltpu.make_async_remote_copy(dst_d, dst_d, sr.at[1, step - 1], rr.at[1, step - 1], device_id={"col": (z + NZ - 1) % NZ}, device_id_type=MESH).wait_recv()

    mine = (z - row + NZ) % NZ
    slot = jnp.minimum(mine, ND - 1)
    lead_out = (x < 2) & (mine < ND)
    o1 = pltpu.make_async_copy(tile.at[pl.ds(0, 32)], ga.at[y, x, slot], lsem.at[4])
    o2 = pltpu.make_async_copy(tile.at[pl.ds(32, 32)], gb.at[x, y, slot], lsem.at[5])

    def zsend(k, d):
        px = x if k < 2 else 3 - x
        dst = ga.at[y, px, slot] if k % 2 == 0 else gb.at[px, y, slot]
        to = {"row": px * 4 + y, "col": (z + d) % NZ}
        return pltpu.make_async_remote_copy(tile.at[pl.ds(32 * k, 32)], dst, sz.at[k, d], rz.at[k % 2, slot], device_id=to, device_id_type=MESH)

    order = [(k, d) for d in (4, 3, 5, 2, 6, 1, 7, 0) for k in (2, 3, 0, 1) if d or k >= 2]

    @pl.when(lead_out)
    def _():
        for k, d in order:
            zsend(k, d).start()
        o1.start()
        o2.start()

    c_row.wait()
    rows_b[...] = rows_f[...].astype(BF16)
    for ref in (ub, ul, rbuf, wprev, xb, yb):
        ref[...] = jnp.zeros_like(ref)

    @pl.when(x < 2)
    def _():
        c1.start()

    @pl.when(lead_out)
    def _():
        o1.wait()
        o2.wait()

    for d in range(ND):
        @pl.when((mine != d) | (x >= 2))
        def _():
            pltpu.make_async_remote_copy(tile.at[pl.ds(0, 32)], ga.at[y, x, d], sz.at[0, 0], rz.at[0, d], device_id={"col": (z + 1) % NZ}, device_id_type=MESH).wait_recv()
            pltpu.make_async_remote_copy(tile.at[pl.ds(32, 32)], gb.at[x, y, d], sz.at[1, 0], rz.at[1, d], device_id={"col": (z + 1) % NZ}, device_id_type=MESH).wait_recv()

    c_col.wait()
    for c in ring(1):
        c.start()
    c_block.start()

    def plane(buf, first, step, up, ss, rs, cut):
        f, s = (x, y) if first else (y, x)
        fd, sd = (xs, ys) if first else (ys, xs)
        if step <= 2:
            base = lambda d: buf.at[s, (f + d) % 4]
            dev = fd
        else:
            base = lambda d: buf.at[(s + d) % 4]
            dev = sd
        me = step - 1
        if step % 2 == 1:
            src, rcv = base(0), base(3 if up else 1)
        else:
            src, rcv = base(3 if up else 1), base(2)
            src, rcv = cut(src, up, step), cut(rcv, up, step)
        k = 0 if up else 1
        to = {"row": dev(1 if up else 3)}
        send = pltpu.make_async_remote_copy(src, src, ss.at[me, k], rs.at[me, k], device_id=to, device_id_type=MESH)
        recv = pltpu.make_async_remote_copy(rcv, rcv, ss.at[me, k], rs.at[me, k], device_id=to, device_id_type=MESH)
        return send, recv

    def cut_lead(ref, up, step):
        h = pl.ds(0 if up else 16, 16)
        return ref.at[:, h] if step == 2 else ref.at[:, :, h]

    def cut_strip(ref, up, step):
        h = pl.ds(0 if up else 16, 16)
        return ref.at[h] if step == 2 else ref.at[:, h]

    def plane_step(step, bufs, ss, rs, cut):
        out = []
        for part in range(2):
            for up in (True, False):
                out.append(plane(bufs[part], part == 0, step, up, ss.at[part], rs.at[part], cut))
        return out

    def own_rows():
        @pl.when(x >= 2)
        def _():
            c1.wait_recv()

        def put(src):
            a = pltpu.make_async_copy(src.at[pl.ds(0, 32)], ra.at[y, x], lsem.at[6])
            b = pltpu.make_async_copy(src.at[pl.ds(32, 32)], rb.at[x, y], lsem.at[7])
            a.start()
            b.start()
            a.wait()
            b.wait()

        @pl.when(x >= 2)
        def _():
            put(rhalf)

        @pl.when(x < 2)
        def _():
            put(rows_b)

    for step in range(1, 5):
        cs = plane_step(step, (ga, gb), sp, rp, cut_lead)
        for s, _ in cs:
            s.start()
        if step == 1:
            own_rows()
            one_hot(rm_ref, team, z, pc.at[0])
        elif step == 3:
            one_hot(rm_ref, team, z + NZ, pc.at[1])
            one_hot(rm_ref, team, pos, pr)
        for _, r in cs:
            r.wait_recv()

    def strip_start(step):
        for s, _ in plane_step(step, (ra, rb), sq, rq, cut_strip):
            s.start()

    def strip_recv(step):
        for _, r in plane_step(step, (ra, rb), sq, rq, cut_strip):
            r.wait_recv()

    def ring_start(step):
        for c in ring(step):
            c.start()

    def progress(J):
        @pl.when(J == 0)
        def _():
            ring_recv(1)
            ring_start(2)

        @pl.when(J == 1)
        def _():
            strip_recv(1)
            strip_start(2)

        @pl.when(J == 2)
        def _():
            strip_recv(2)
            strip_start(3)
            ring_recv(2)
            ring_start(3)

        @pl.when(J == 4)
        def _():
            strip_recv(3)
            strip_start(4)
            ring_recv(3)
            ring_start(4)

    strip_start(1)
    assemble(ga, gb, u_ref)

    def ready():
        strip_recv(4)
        ring_recv(4)

    def pair_copies(c, n):
        ks = pl.ds(2 * n, 2)
        far = pltpu.make_async_remote_copy(placed.at[c, ks], other_out.at[c, ks], st.at[c, n], rt.at[c, n], device_id={"team": 1 - team}, device_id_type=MESH)
        near = pltpu.make_async_copy(placed.at[c, ks], own_out.at[c, ks], lt.at[c, n])
        return far, near

    pending = []

    def flush():
        for pair in pending:
            for copy in pair_copies(*pair):
                copy.start()
        pending.clear()

    def send(c, n):
        flush()
        pending.append((c, n))

    core(pos, ab, ra, rb, zs, u_ref, ub, ul, w_ref, dref, rbuf, wprev, xb, yb, upd, tmp, pr, pc, placed,
         progress, ready, c_block.wait, c_out.start, send)
    flush()

    for step in range(1, 5):
        for s, _ in plane_step(step, (ga, gb), sp, rp, cut_lead) + plane_step(step, (ra, rb), sq, rq, cut_strip):
            s.wait_send()
        for c in ring(step):
            c.wait_send()

    for c in range(2):
        for n in range(3):
            far, near = pair_copies(c, n)
            far.wait()
            near.wait()
    c_out.wait()

    @pl.when(x < 2)
    def _():
        c1.wait_send()

    @pl.when(lead_out)
    def _():
        for k, d in order:
            zsend(k, d).wait_send()


def factor_block(block):
    sub = lax.broadcasted_iota(jnp.int32, (8, T), 0)
    lane = lax.broadcasted_iota(jnp.int32, (8, T), 1)
    V = [block[8 * s : 8 * s + 8, :] for s in range(16)]
    W = [jnp.where(lane == sub + 8 * s, 1.0, 0.0).astype(F32) for s in range(16)]
    lb = lambda v, j: jnp.broadcast_to(v[:, j : j + 1], (8, T))
    sb = lambda v, k: jnp.broadcast_to(v[k : k + 1, :], (8, T))
    for t in range(16):
        v, w = V[t], W[t]
        C = [lb(v, 8 * t + j) for j in range(8)]
        rv, rw, rs, uk = [], [], [], []
        for k in range(8):
            r = lax.rsqrt(sb(C[k], k))
            a, b = sb(v, k) * r, sb(w, k) * r
            m = jnp.where(sub > k, C[k] * r, 0.0)
            us = {}
            for j in range(k + 1, 8):
                us[j] = sb(C[j], k) * r
                C[j] = C[j] - m * us[j]
            v = jnp.where(sub == k, a, v - m * a)
            w = jnp.where(sub == k, b, w - m * b)
            rv.append(a)
            rw.append(b)
            rs.append(r)
            uk.append(us)
        V[t], W[t] = v, w
        for s in range(t + 1, 16):
            Cs = [lb(V[s], 8 * t + j) for j in range(8)]
            vs, ws = V[s], W[s]
            for k in range(8):
                m = Cs[k] * rs[k]
                for j in range(k + 1, 8):
                    Cs[j] = Cs[j] - m * uk[k][j]
                vs = vs - m * rv[k]
                ws = ws - m * rw[k]
            V[s], W[s] = vs, ws
    return jnp.concatenate(W, axis=0)


def assemble(ga, gb, u_ref):
    for i in range(NB):
        y = i % 4
        top, bot = (0, 3) if i < 4 else (1, 2)
        for d in range(ND):
            j = (i + d) % NB
            if d == 4 and i >= 4:
                continue
            parts = [ga[y, top, d], gb[top, y, d], ga[y, bot, d], gb[bot, y, d]]
            if j >= i:
                for k in range(4):
                    u_ref[i * T + 32 * k : i * T + 32 * k + 32, j * T : j * T + T] = parts[k]
            else:
                u_ref[j * T : j * T + T, i * T : i * T + T] = jnp.concatenate(parts, axis=0).T
    for i in range(1, NB):
        u_ref[i * T : i * T + T, 0 : i * T] = jnp.zeros((T, i * T), F32)


def lead_step(J, depth, c0, u_ref, uh, ul, w_ref, dref, rbuf, wprev, filler):
    last = isinstance(J, int)
    wide = LEAD - c0
    cols = pl.ds(c0, wide)
    j0 = pl.multiple_of(J * T, T)
    p0 = pl.multiple_of(jnp.maximum(J - 1, 0) * T, T)
    n0 = pl.multiple_of(jnp.minimum(J + 1, NB - 1) * T, T)
    col = lax.broadcasted_iota(jnp.int32, (T, wide), 1) + c0
    sub = lax.broadcasted_iota(jnp.int32, (T, wide), 0)
    filler()
    row = jnp.where(col >= sub + p0, dot3(wprev[...], rbuf[:, cols], NN), 0.0)
    hi, lo = split(row)
    uh[pl.ds(p0, T), cols] = hi
    ul[pl.ds(p0, T), cols] = lo

    def ahead(mine, them):
        mh, ml, th, tl = uh[:depth, mine], ul[:depth, mine], uh[:depth, them], ul[:depth, them]
        return dot1(mh, th, TN) + dot1(mh, tl, TN) + dot1(ml, th, TN)

    if not last:
        rbuf[:, cols] = u_ref[pl.ds(j0, T), cols] - ahead(pl.ds(j0, T), cols)
        nxt = u_ref[pl.ds(n0, T), pl.ds(n0, T)] - ahead(pl.ds(n0, T), pl.ds(n0, T))
    inv = factor_block(dref[...])
    w_ref[J] = inv
    if not last:
        wprev[...] = inv
        edge = dot3(inv, rbuf[:, pl.ds(n0, T)], NN)
        dref[...] = nxt - dot3(edge, edge, TN)


def one_hot(rm_ref, team, first, out):
    sub = lax.broadcasted_iota(jnp.int32, (ROWS, T), 0)
    for s in range(RT):
        tile = s * 16 + first
        both = rm_ref[:, pl.ds(pl.multiple_of(jnp.maximum(tile - NB, 0) * T, T), T)]
        line = jnp.where(team == 0, both[0:1], both[1:2])
        spot = jnp.where(tile >= NB, (line // 2048) * T + line % T, -1)
        out[:, s * T : s * T + T] = jnp.where(sub == spot, 1.0, 0.0).astype(BF16)


def solve(J, depth, pos, ra, rb, zs, ub, w_ref, xb, yb):
    j0 = pl.multiple_of(J * T, T)
    cs = pl.ds(j0, T)
    acc = zs[J]
    if depth:
        acc = acc - dot1(xb[:, :depth], ub[:depth, cs], NN)
    xj = dot3(acc, w_ref[J], NT)
    r = lax.broadcasted_iota(jnp.int32, (T, T), 0)
    c = lax.broadcasted_iota(jnp.int32, (T, T), 1)
    xb[T:, cs] = xj[T:].astype(BF16)
    xb[:T, cs] = jnp.where(pos * T + r >= j0 + c, xj[:T], 0.0).astype(BF16)
    y, top = J % 4, J // 4
    acc = jnp.concatenate([ra[y, top], rb[top, y], ra[y, 3 - top], rb[3 - top, y]], axis=0).astype(F32)
    if depth:
        acc = acc - dot1(ub[:depth, cs], yb[:depth, :], TN)
    yb[cs, :] = dot3(w_ref[J], acc, NN).astype(BF16)


def place(pr, pc, upd, tmp, placed, send):
    for c in range(2):
        for n in range(3):
            cs = slice(n * 256, n * 256 + 256)
            tmp[c, :, cs] = dot1(pr[...], upd[c, :, cs], NN).astype(BF16)
        for n in range(3):
            out = dot1(tmp[c], pc[c, n * 256 : n * 256 + 256, :], NT).astype(BF16)
            placed[c, 2 * n] = out[:, :T]
            placed[c, 2 * n + 1] = out[:, T:]
            send(c, n)


def core(pos, ab, ra, rb, zs, u_ref, ub, ul, w_ref, dref, rbuf, wprev, xb, yb, upd, tmp, pr, pc, placed, progress, ready, block_ready, solved, send):
    lead = (u_ref, ub, ul, w_ref, dref, rbuf, wprev)
    dref[...] = u_ref[:T, :T]

    def early(J, _):
        progress(J)
        lead_step(J, 4 * T, 0, *lead, lambda: None)
        return 0

    lax.fori_loop(0, 5, early, 0)
    ready()
    args = (pos, ra, rb, zs, ub, w_ref, xb, yb)

    def late(J, _):
        def filler():
            for k in range(3):
                solve(3 * (J - 5) + k, 5 * T, *args)

        lead_step(J, 6 * T, 4 * T, *lead, filler)
        return 0

    lax.fori_loop(5, 7, late, 0)
    block_ready()

    def last():
        for n in range(6):
            cs = slice(n * 256, n * 256 + 256)
            ab[:, cs] = ab[:, cs] - dot1(xb[:, : 6 * T], yb[: 6 * T, cs], NN)
        solve(6, 6 * T, *args)

    lead_step(7, 7 * T, 6 * T, *lead, last)
    solve(7, 7 * T, *args)
    solved()
    for n in range(6):
        cs = slice(n * 256, n * 256 + 256)
        v = (ab[:, cs] - dot1(xb[:, 6 * T :], yb[6 * T :, cs], NN)).astype(BF16)
        upd[0, :, n * T : n * T + T] = v[:, :T]
        upd[1, :, n * T : n * T + T] = v[:, T:]
    place(pr, pc, upd, tmp, placed, send)


def panels(front, rm):
    vm = pl.BlockSpec(memory_space=pltpu.VMEM)
    hbm = pl.BlockSpec(memory_space=pl.ANY)
    dma = pltpu.SemaphoreType.DMA
    v = pltpu.VMEM
    return pl.pallas_call(
        panel_kernel,
        out_shape=(
            jax.ShapeDtypeStruct((ROWS, LEAD), BF16),
            jax.ShapeDtypeStruct((2, RT, ROWS, T), BF16),
            jax.ShapeDtypeStruct((2, RT, ROWS, T), BF16),
        ),
        in_specs=[hbm, vm],
        out_specs=(hbm,) * 3,
        scratch_shapes=[
            v((ROWS, COLS), F32), v((4, 4, 32, COLS), BF16), v((4, 4, 32, COLS), BF16), v((NZ, ROWS, T), F32),
            v((LEAD, LEAD), F32), v((LEAD, LEAD), BF16), v((LEAD, LEAD), BF16), v((NB, T, T), F32),
            v((T, T), F32), v((T, LEAD), F32), v((T, T), F32), v((ROWS, LEAD), BF16), v((LEAD, COLS), BF16),
            v((2, ROWS, ROWS), BF16), v((2, ROWS, ROWS), BF16), v((ROWS, ROWS), BF16), v((2, ROWS, ROWS), BF16), v((2, RT, ROWS, T), BF16),
            v((4, 4, ND, 32, T), F32), v((4, 4, ND, 32, T), F32),
            v((T, COLS), F32), v((T, COLS), BF16), v((T, T), F32), v((64, COLS), BF16),
            dma((10,)), dma((2,)), dma((2,)), dma((4, NZ)), dma((2, ND)),
            dma((2, 4, 2)), dma((2, 4, 2)), dma((2, 4, 2)), dma((2, 4, 2)), dma((2, 4)), dma((2, 4)),
            dma((2, 3)), dma((2, 3)), dma((2, 3)),
        ],
        compiler_params=pltpu.CompilerParams(collective_id=0, has_side_effects=True, vmem_limit_bytes=VMEM_LIMIT),
        name="panels",
    )(front, rm)


def finish_kernel(owner_ref, own, other, xb, fac, out):
    team = lax.axis_index("team")
    pos = lax.axis_index("row")
    fac[0] = xb[...].astype(F32)
    for s in range(RT):
        keep = owner_ref[s * 16 + pos] == team
        rows = slice(s * T, s * T + T)
        for c in range(2):
            total = own[c, 0, rows].astype(F32) + other[c, 0, rows].astype(F32)
            out[0, rows, c * T : c * T + T] = jnp.where(keep, total, 0.0)


def finish(tile_owner, own, other, xb):
    tiles = pl.BlockSpec((2, 1, ROWS, T), lambda k: (0, k, 0, 0))
    return pl.pallas_call(
        finish_kernel,
        grid=(RT,),
        out_shape=(jax.ShapeDtypeStruct((1, ROWS, LEAD), F32), jax.ShapeDtypeStruct((1, ROWS, COLS), F32)),
        in_specs=[pl.BlockSpec(memory_space=pltpu.SMEM), tiles, tiles, pl.BlockSpec((T, LEAD), lambda k: (k, 0))],
        out_specs=(pl.BlockSpec((1, T, LEAD), lambda k: (0, k, 0)), pl.BlockSpec((1, ROWS, 2 * T), lambda k: (0, 0, k))),
        name="finish",
    )(tile_owner, own, other, xb)


def shards(front, row_map, tile_owner):
    xb, own, other = panels(front, row_map)
    return finish(tile_owner, own, other, xb)


def solution(mesh):
    return jax.shard_map(
        shards,
        mesh=mesh,
        in_specs=(P("team", "row", "col"), P(), P()),
        out_specs=(P("team", "row", None), P("team", "row", "col")),
        check_vma=False,
    )
```

```python
import jax
import jax.numpy as jnp
from jax import lax
from jax.experimental import pallas as pl
from jax.experimental.pallas import tpu as pltpu
from jax.sharding import PartitionSpec as P

T = 128
LEAD = 1024
NB = 8
RT = 6
CT = 12
ROWS = RT * T
COLS = CT * T
NZ = 8
ND = 5
MESH = pl.DeviceIdType.MESH
VMEM_LIMIT = 60 << 20
F32 = jnp.float32
BF16 = jnp.bfloat16
NN = (((1,), (0,)), ((), ()))
NT = (((1,), (1,)), ((), ()))
TN = (((0,), (0,)), ((), ()))


def dot1(a, b, dims):
    return lax.dot_general(a, b, dims, preferred_element_type=F32)


def split(a):
    hi = a.astype(BF16)
    return hi, (a - hi.astype(F32)).astype(BF16)


def dot3(a, b, dims):
    ah, al = split(a)
    bh, bl = split(b)
    return dot1(ah, bh, dims) + dot1(ah, bl, dims) + dot1(al, bh, dims)


def row_of(x, y):
    return y + jnp.where((x == 0) | (x == 3), 0, 4)


def panel_kernel(front, rm_ref, x_out, own_out, other_out,
                 ab, ra, rb, zs, u_ref, ub, ul, w_ref, dref, rbuf, wprev, xb, yb, upd, tmp, pr, pc, placed,
                 ga, gb, rows_f, rows_b, tile, rhalf,
                 lsem, s0, r0, sz, rz, sp, rp, sq, rq, sr, rr, st, rt, lt):
    team = lax.axis_index("team")
    pos = lax.axis_index("row")
    z = lax.axis_index("col")
    x, y = pos // 4, pos % 4
    xs = lambda d: ((x + d) % 4) * 4 + y
    ys = lambda d: x * 4 + (y + d) % 4
    row = row_of(x, y)

    c_col = pltpu.make_async_copy(front.at[0, :, pl.ds(0, T)], zs.at[z], lsem.at[0])
    c_row = pltpu.make_async_copy(front.at[0, pl.ds(0, T), :], rows_f, lsem.at[1])
    c_tile = pltpu.make_async_copy(front.at[0, pl.ds(0, T), pl.ds(0, T)], tile, lsem.at[2])
    c_tile.start()
    c_row.start()
    c_col.start()
    c_block = pltpu.make_async_copy(front.at[0], ab, lsem.at[8])
    c_out = pltpu.make_async_copy(xb, x_out, lsem.at[9])

    bar = pltpu.get_barrier_semaphore()
    for d in (1, 3):
        pl.semaphore_signal(bar, inc=1, device_id={"row": xs(d)}, device_id_type=MESH)
        pl.semaphore_signal(bar, inc=1, device_id={"row": ys(d)}, device_id_type=MESH)
    for d in range(1, NZ):
        pl.semaphore_signal(bar, inc=1, device_id={"col": (z + d) % NZ}, device_id_type=MESH)
    pl.semaphore_signal(bar, inc=1, device_id={"team": 1 - team}, device_id_type=MESH)
    for ref in (ub, ul, rbuf, wprev, xb, yb):
        ref[...] = jnp.zeros_like(ref)
    for d in range(1, NZ):
        pl.semaphore_signal(bar, inc=1, device_id={"row": (3 - x) * 4 + y, "col": (z + d) % NZ}, device_id_type=MESH)
    c_tile.wait()
    pl.semaphore_wait(bar, 4 + NZ + NZ - 1)

    mirror = {"row": (3 - x) * 4 + y}
    c1 = pltpu.make_async_remote_copy(rows_b.at[pl.ds(64, 64)], rhalf, s0.at[1], r0.at[1], device_id=mirror, device_id_type=MESH)

    def ring(step):
        up, dn = (z - step + 1 + NZ) % NZ, (z + step - 1) % NZ
        if step < 4:
            src_u, src_d = zs.at[up], zs.at[dn]
        else:
            src_u, src_d = zs.at[up, pl.ds(0, ROWS // 2)], zs.at[dn, pl.ds(ROWS // 2, ROWS // 2)]
        a = pltpu.make_async_remote_copy(src_u, src_u, sr.at[0, step - 1], rr.at[0, step - 1], device_id={"col": (z + 1) % NZ}, device_id_type=MESH)
        b = pltpu.make_async_remote_copy(src_d, src_d, sr.at[1, step - 1], rr.at[1, step - 1], device_id={"col": (z + NZ - 1) % NZ}, device_id_type=MESH)
        return a, b

    def ring_recv(step):
        up, dn = (z - step + NZ) % NZ, (z + step) % NZ
        if step < 4:
            dst_u, dst_d = zs.at[up], zs.at[dn]
        else:
            dst_u, dst_d = zs.at[up, pl.ds(0, ROWS // 2)], zs.at[dn, pl.ds(ROWS // 2, ROWS // 2)]
        pltpu.make_async_remote_copy(dst_u, dst_u, sr.at[0, step - 1], rr.at[0, step - 1], device_id={"col": (z + 1) % NZ}, device_id_type=MESH).wait_recv()
        pltpu.make_async_remote_copy(dst_d, dst_d, sr.at[1, step - 1], rr.at[1, step - 1], device_id={"col": (z + NZ - 1) % NZ}, device_id_type=MESH).wait_recv()

    mine = (z - row + NZ) % NZ
    slot = jnp.minimum(mine, ND - 1)
    lead_out = (x < 2) & (mine < ND)
    o1 = pltpu.make_async_copy(tile.at[pl.ds(0, 32)], ga.at[y, x, slot], lsem.at[4])
    o2 = pltpu.make_async_copy(tile.at[pl.ds(32, 32)], gb.at[x, y, slot], lsem.at[5])

    def zsend(k, d):
        px = x if k < 2 else 3 - x
        dst = ga.at[y, px, slot] if k % 2 == 0 else gb.at[px, y, slot]
        to = {"row": px * 4 + y, "col": (z + d) % NZ}
        return pltpu.make_async_remote_copy(tile.at[pl.ds(32 * k, 32)], dst, sz.at[k, d], rz.at[k % 2, slot], device_id=to, device_id_type=MESH)

    order = [(k, d) for d in (4, 3, 5, 2, 6, 1, 7, 0) for k in (2, 3, 0, 1) if d or k >= 2]

    @pl.when(lead_out)
    def _():
        for k, d in order:
            zsend(k, d).start()
        o1.start()
        o2.start()

    c_row.wait()
    rows_b[...] = rows_f[...].astype(BF16)
    for ref in (ub, ul, rbuf, wprev, xb, yb):
        ref[...] = jnp.zeros_like(ref)

    @pl.when(x < 2)
    def _():
        c1.start()

    @pl.when(lead_out)
    def _():
        o1.wait()
        o2.wait()

    for d in range(ND):
        @pl.when((mine != d) | (x >= 2))
        def _():
            pltpu.make_async_remote_copy(tile.at[pl.ds(0, 32)], ga.at[y, x, d], sz.at[0, 0], rz.at[0, d], device_id={"col": (z + 1) % NZ}, device_id_type=MESH).wait_recv()
            pltpu.make_async_remote_copy(tile.at[pl.ds(32, 32)], gb.at[x, y, d], sz.at[1, 0], rz.at[1, d], device_id={"col": (z + 1) % NZ}, device_id_type=MESH).wait_recv()

    c_col.wait()
    for c in ring(1):
        c.start()
    c_block.start()

    def plane(buf, first, step, up, ss, rs, cut):
        f, s = (x, y) if first else (y, x)
        fd, sd = (xs, ys) if first else (ys, xs)
        if step <= 2:
            base = lambda d: buf.at[s, (f + d) % 4]
            dev = fd
        else:
            base = lambda d: buf.at[(s + d) % 4]
            dev = sd
        me = step - 1
        if step % 2 == 1:
            src, rcv = base(0), base(3 if up else 1)
        else:
            src, rcv = base(3 if up else 1), base(2)
            src, rcv = cut(src, up, step), cut(rcv, up, step)
        k = 0 if up else 1
        to = {"row": dev(1 if up else 3)}
        send = pltpu.make_async_remote_copy(src, src, ss.at[me, k], rs.at[me, k], device_id=to, device_id_type=MESH)
        recv = pltpu.make_async_remote_copy(rcv, rcv, ss.at[me, k], rs.at[me, k], device_id=to, device_id_type=MESH)
        return send, recv

    def cut_lead(ref, up, step):
        h = pl.ds(0 if up else 16, 16)
        return ref.at[:, h] if step == 2 else ref.at[:, :, h]

    def plane_step(step, bufs, ss, rs, cut):
        out = []
        for part in range(2):
            for up in (True, False):
                out.append(plane(bufs[part], part == 0, step, up, ss.at[part], rs.at[part], cut))
        return out

    def own_rows():
        @pl.when(x >= 2)
        def _():
            c1.wait_recv()

        def put(src):
            a = pltpu.make_async_copy(src.at[pl.ds(0, 32)], ra.at[y, x], lsem.at[6])
            b = pltpu.make_async_copy(src.at[pl.ds(32, 32)], rb.at[x, y], lsem.at[7])
            a.start()
            b.start()
            a.wait()
            b.wait()

        @pl.when(x >= 2)
        def _():
            put(rhalf)

        @pl.when(x < 2)
        def _():
            put(rows_b)

    def strip(kind, off=0):
        out = []
        for part, buf in enumerate((ra, rb)):
            f, s, fd, sd = (x, y, xs, ys) if part == 0 else (y, x, ys, xs)
            spot = lambda ds, df: buf.at[(s + ds) % 4, (f + df) % 4]
            for k in range(2):
                h = pl.ds(16 * k, 16)
                back = 1 if k else 3
                src, dst = {
                    1: lambda: (spot(0, 0), spot(0, back)),
                    2: lambda: (spot(0, back).at[h], spot(0, 2).at[h]),
                    3: lambda: (spot(0, off), spot(back, off)),
                    4: lambda: (spot(back, off).at[h], spot(2, off).at[h]),
                }[kind]()
                to = {"row": (fd if kind < 3 else sd)(4 - back)}
                sem = (kind - 1) if kind < 3 else 2 + 4 * (kind - 3) + off
                out.append((
                    pltpu.make_async_remote_copy(src, src, sq.at[part, sem, k], rq.at[part, sem, k], device_id=to, device_id_type=MESH),
                    pltpu.make_async_remote_copy(dst, dst, sq.at[part, sem, k], rq.at[part, sem, k], device_id=to, device_id_type=MESH),
                ))
        return out

    def strip_start(*args):
        for s, _ in strip(*args):
            s.start()

    def strip_recv(*args):
        for _, r in strip(*args):
            r.wait_recv()

    def ring_start(step):
        for c in ring(step):
            c.start()

    for step in range(1, 5):
        cs = plane_step(step, (ga, gb), sp, rp, cut_lead)
        for s, _ in cs:
            s.start()
        if step == 4:
            strip_start(1)
            strip_start(3, 0)
            ring_recv(1)
            ring_start(2)
        if step == 1:
            own_rows()
            one_hot(rm_ref, team, z, pc.at[0])
        elif step == 3:
            one_hot(rm_ref, team, z + NZ, pc.at[1])
            one_hot(rm_ref, team, pos, pr)
        for _, r in cs:
            r.wait_recv()

    def progress(J):
        @pl.when(J == 1)
        def _():
            strip_recv(1)
            strip_start(2)
            strip_recv(3, 0)
            strip_start(3, 1)
            strip_start(3, 3)
            strip_start(4, 0)
            ring_recv(2)
            ring_start(3)

        @pl.when(J == 2)
        def _():
            strip_recv(2)
            strip_start(3, 2)
            strip_recv(3, 1)
            strip_recv(3, 3)
            strip_start(4, 1)
            strip_start(4, 3)

        @pl.when(J == 3)
        def _():
            strip_recv(3, 2)
            strip_start(4, 2)

        @pl.when(J == 4)
        def _():
            ring_recv(3)
            ring_start(4)

    assemble(ga, gb, u_ref)

    def ready():
        for off in range(4):
            strip_recv(4, off)

    def ring_ready():
        ring_recv(4)

    def pair_copies(c, n):
        ks = pl.ds(2 * n, 2)
        far = pltpu.make_async_remote_copy(placed.at[c, ks], other_out.at[c, ks], st.at[c, n], rt.at[c, n], device_id={"team": 1 - team}, device_id_type=MESH)
        near = pltpu.make_async_copy(placed.at[c, ks], own_out.at[c, ks], lt.at[c, n])
        return far, near

    pending = []

    def flush():
        for pair in pending:
            for copy in pair_copies(*pair):
                copy.start()
        pending.clear()

    def send(c, n):
        flush()
        pending.append((c, n))

    core(pos, ab, ra, rb, zs, u_ref, ub, ul, w_ref, dref, rbuf, wprev, xb, yb, upd, tmp, pr, pc, placed,
         progress, ready, ring_ready, c_block.wait, c_out.start, send)
    flush()

    for step in range(1, 5):
        for s, _ in plane_step(step, (ga, gb), sp, rp, cut_lead):
            s.wait_send()
        for c in ring(step):
            c.wait_send()

    for kind, off in [(1, 0), (2, 0)] + [(k, o) for k in (3, 4) for o in range(4)]:
        for s, _ in strip(kind, off):
            s.wait_send()

    for c in range(2):
        for n in range(3):
            far, near = pair_copies(c, n)
            far.wait()
            near.wait()
    c_out.wait()

    @pl.when(x < 2)
    def _():
        c1.wait_send()

    @pl.when(lead_out)
    def _():
        for k, d in order:
            zsend(k, d).wait_send()


def factor_block(block):
    sub = lax.broadcasted_iota(jnp.int32, (8, T), 0)
    lane = lax.broadcasted_iota(jnp.int32, (8, T), 1)
    V = [block[8 * s : 8 * s + 8, :] for s in range(16)]
    W = [jnp.where(lane == sub + 8 * s, 1.0, 0.0).astype(F32) for s in range(16)]
    lb = lambda v, j: jnp.broadcast_to(v[:, j : j + 1], (8, T))
    sb = lambda v, k: jnp.broadcast_to(v[k : k + 1, :], (8, T))
    for t in range(16):
        v, w = V[t], W[t]
        C = [lb(v, 8 * t + j) for j in range(8)]
        rv, rw, rs, uk = [], [], [], []
        for k in range(8):
            r = lax.rsqrt(sb(C[k], k))
            a, b = sb(v, k) * r, sb(w, k) * r
            m = jnp.where(sub > k, C[k] * r, 0.0)
            us = {}
            for j in range(k + 1, 8):
                us[j] = sb(C[j], k) * r
                C[j] = C[j] - m * us[j]
            v = jnp.where(sub == k, a, v - m * a)
            w = jnp.where(sub == k, b, w - m * b)
            rv.append(a)
            rw.append(b)
            rs.append(r)
            uk.append(us)
        V[t], W[t] = v, w
        for s in range(t + 1, 16):
            Cs = [lb(V[s], 8 * t + j) for j in range(8)]
            vs, ws = V[s], W[s]
            for k in range(8):
                m = Cs[k] * rs[k]
                for j in range(k + 1, 8):
                    Cs[j] = Cs[j] - m * uk[k][j]
                vs = vs - m * rv[k]
                ws = ws - m * rw[k]
            V[s], W[s] = vs, ws
    return jnp.concatenate(W, axis=0)


def assemble(ga, gb, u_ref):
    for i in range(NB):
        y = i % 4
        top, bot = (0, 3) if i < 4 else (1, 2)
        for d in range(ND):
            j = (i + d) % NB
            if d == 4 and i >= 4:
                continue
            parts = [ga[y, top, d], gb[top, y, d], ga[y, bot, d], gb[bot, y, d]]
            if j >= i:
                for k in range(4):
                    u_ref[i * T + 32 * k : i * T + 32 * k + 32, j * T : j * T + T] = parts[k]
            else:
                u_ref[j * T : j * T + T, i * T : i * T + T] = jnp.concatenate(parts, axis=0).T
    for i in range(1, NB):
        u_ref[i * T : i * T + T, 0 : i * T] = jnp.zeros((T, i * T), F32)


def at(J):
    return J * T if isinstance(J, int) else pl.multiple_of(J * T, T)


def lead_step(J, depth, c0, u_ref, uh, ul, w_ref, dref, rbuf, wprev, filler):
    fixed = isinstance(J, int)
    last = fixed and J == NB - 1
    wide = LEAD - c0
    cols = pl.ds(c0, wide)
    j0 = at(J)
    p0 = at(J - 1 if fixed else jnp.maximum(J - 1, 0))
    n0 = at(min(J + 1, NB - 1) if fixed else jnp.minimum(J + 1, NB - 1))
    col = lax.broadcasted_iota(jnp.int32, (T, wide), 1) + c0
    sub = lax.broadcasted_iota(jnp.int32, (T, wide), 0)
    filler()
    row = jnp.where(col >= sub + p0, dot3(wprev[...], rbuf[:, cols], NN), 0.0)
    hi, lo = split(row)
    uh[pl.ds(p0, T), cols] = hi
    ul[pl.ds(p0, T), cols] = lo

    def ahead(mine, them):
        mh, ml, th, tl = uh[:depth, mine], ul[:depth, mine], uh[:depth, them], ul[:depth, them]
        return dot1(mh, th, TN) + dot1(mh, tl, TN) + dot1(ml, th, TN)

    if not last:
        rbuf[:, cols] = u_ref[pl.ds(j0, T), cols] - ahead(pl.ds(j0, T), cols)
        nxt = u_ref[pl.ds(n0, T), pl.ds(n0, T)] - ahead(pl.ds(n0, T), pl.ds(n0, T))
    inv = factor_block(dref[...])
    w_ref[J] = inv
    if not last:
        wprev[...] = inv
        edge = dot3(inv, rbuf[:, pl.ds(n0, T)], NN)
        dref[...] = nxt - dot3(edge, edge, TN)


def one_hot(rm_ref, team, first, out):
    sub = lax.broadcasted_iota(jnp.int32, (ROWS, T), 0)
    for s in range(RT):
        tile = s * 16 + first
        both = rm_ref[:, pl.ds(pl.multiple_of(jnp.maximum(tile - NB, 0) * T, T), T)]
        line = jnp.where(team == 0, both[0:1], both[1:2])
        spot = jnp.where(tile >= NB, (line // 2048) * T + line % T, -1)
        out[:, s * T : s * T + T] = jnp.where(sub == spot, 1.0, 0.0).astype(BF16)


def solve_rows(J, pos, zs, ub, w_ref, xb):
    d = J * T
    cs = slice(d, d + T)
    acc = zs[J]
    if d:
        acc = acc - dot1(xb[:, :d], ub[:d, cs], NN)
    xj = dot3(acc, w_ref[J], NT)
    r = lax.broadcasted_iota(jnp.int32, (T, T), 0)
    c = lax.broadcasted_iota(jnp.int32, (T, T), 1)
    xb[T:, cs] = xj[T:].astype(BF16)
    xb[:T, cs] = jnp.where(pos * T + r >= d + c, xj[:T], 0.0).astype(BF16)


def solve_cols(J, ra, rb, ub, w_ref, yb):
    d = J * T
    cs = slice(d, d + T)
    y, top = J % 4, J // 4
    acc = jnp.concatenate([ra[y, top], rb[top, y], ra[y, 3 - top], rb[3 - top, y]], axis=0).astype(F32)
    if d:
        acc = acc - dot1(ub[:d, cs], yb[:d, :], TN)
    yb[cs, :] = dot3(w_ref[J], acc, NN).astype(BF16)


def place(pr, pc, upd, tmp, placed, send):
    for c in range(2):
        for n in range(3):
            tmp[c, n] = dot1(upd[c], pc[c, n * 256 : n * 256 + 256, :], NT).astype(BF16)
            out = dot1(pr[...], tmp[c, n], NN).astype(BF16)
            placed[c, 2 * n] = out[:, :T]
            placed[c, 2 * n + 1] = out[:, T:]
            send(c, n)


def core(pos, ab, ra, rb, zs, u_ref, ub, ul, w_ref, dref, rbuf, wprev, xb, yb, upd, tmp, pr, pc, placed, progress, ready, ring_ready, block_ready, solved, send):
    lead = (u_ref, ub, ul, w_ref, dref, rbuf, wprev)
    dref[...] = u_ref[:T, :T]

    def early(J, _):
        progress(J)
        lead_step(J, 4 * T, 0, *lead, lambda: None)
        return 0

    lax.fori_loop(0, 5, early, 0)
    rows = lambda *js: [solve_rows(j, pos, zs, ub, w_ref, xb) for j in js]
    columns = lambda *js: [solve_cols(j, ra, rb, ub, w_ref, yb) for j in js]
    ready()
    lead_step(5, 5 * T, 5 * T, *lead, lambda: columns(0, 1, 2, 3))
    ring_ready()
    lead_step(6, 6 * T, 5 * T, *lead, lambda: (rows(0, 1, 2, 3, 4, 5), columns(4, 5)))
    block_ready()

    def last():
        for n in range(6):
            cs = slice(n * 256, n * 256 + 256)
            ab[:, cs] = ab[:, cs] - dot1(xb[:, : 6 * T], yb[: 6 * T, cs], NN)
        rows(6)
        columns(6)

    lead_step(7, 7 * T, 6 * T, *lead, last)
    rows(7)
    columns(7)
    solved()
    for n in range(6):
        cs = slice(n * 256, n * 256 + 256)
        v = (ab[:, cs] - dot1(xb[:, 6 * T :], yb[6 * T :, cs], NN)).astype(BF16)
        upd[0, :, n * T : n * T + T] = v[:, :T]
        upd[1, :, n * T : n * T + T] = v[:, T:]
    place(pr, pc, upd, tmp, placed, send)


def panels(front, rm):
    vm = pl.BlockSpec(memory_space=pltpu.VMEM)
    hbm = pl.BlockSpec(memory_space=pl.ANY)
    dma = pltpu.SemaphoreType.DMA
    v = pltpu.VMEM
    return pl.pallas_call(
        panel_kernel,
        out_shape=(
            jax.ShapeDtypeStruct((ROWS, LEAD), BF16),
            jax.ShapeDtypeStruct((2, RT, ROWS, T), BF16),
            jax.ShapeDtypeStruct((2, RT, ROWS, T), BF16),
        ),
        in_specs=[hbm, vm],
        out_specs=(hbm,) * 3,
        scratch_shapes=[
            v((ROWS, COLS), F32), v((4, 4, 32, COLS), BF16), v((4, 4, 32, COLS), BF16), v((NZ, ROWS, T), F32),
            v((LEAD, LEAD), F32), v((LEAD, LEAD), BF16), v((LEAD, LEAD), BF16), v((NB, T, T), F32),
            v((T, T), F32), v((T, LEAD), F32), v((T, T), F32), v((ROWS, LEAD), BF16), v((LEAD, COLS), BF16),
            v((2, ROWS, ROWS), BF16), v((2, 3, ROWS, 256), BF16), v((ROWS, ROWS), BF16), v((2, ROWS, ROWS), BF16), v((2, RT, ROWS, T), BF16),
            v((4, 4, ND, 32, T), F32), v((4, 4, ND, 32, T), F32),
            v((T, COLS), F32), v((T, COLS), BF16), v((T, T), F32), v((64, COLS), BF16),
            dma((10,)), dma((2,)), dma((2,)), dma((4, NZ)), dma((2, ND)),
            dma((2, 4, 2)), dma((2, 4, 2)), dma((2, 10, 2)), dma((2, 10, 2)), dma((2, 4)), dma((2, 4)),
            dma((2, 3)), dma((2, 3)), dma((2, 3)),
        ],
        compiler_params=pltpu.CompilerParams(collective_id=0, has_side_effects=True, vmem_limit_bytes=VMEM_LIMIT),
        name="panels",
    )(front, rm)


def finish_kernel(owner_ref, own, other, xb, fac, out):
    team = lax.axis_index("team")
    pos = lax.axis_index("row")
    fac[0] = xb[...].astype(F32)
    for s in range(RT):
        keep = owner_ref[s * 16 + pos] == team
        rows = slice(s * T, s * T + T)
        for c in range(2):
            total = own[c, 0, rows].astype(F32) + other[c, 0, rows].astype(F32)
            out[0, rows, c * T : c * T + T] = jnp.where(keep, total, 0.0)


def finish(tile_owner, own, other, xb):
    tiles = pl.BlockSpec((2, 1, ROWS, T), lambda k: (0, k, 0, 0))
    return pl.pallas_call(
        finish_kernel,
        grid=(RT,),
        out_shape=(jax.ShapeDtypeStruct((1, ROWS, LEAD), F32), jax.ShapeDtypeStruct((1, ROWS, COLS), F32)),
        in_specs=[pl.BlockSpec(memory_space=pltpu.SMEM), tiles, tiles, pl.BlockSpec((T, LEAD), lambda k: (k, 0))],
        out_specs=(pl.BlockSpec((1, T, LEAD), lambda k: (0, k, 0)), pl.BlockSpec((1, ROWS, 2 * T), lambda k: (0, 0, k))),
        name="finish",
    )(tile_owner, own, other, xb)


def shards(front, row_map, tile_owner):
    xb, own, other = panels(front, row_map)
    return finish(tile_owner, own, other, xb)


def solution(mesh):
    return jax.shard_map(
        shards,
        mesh=mesh,
        in_specs=(P("team", "row", "col"), P(), P()),
        out_specs=(P("team", "row", None), P("team", "row", "col")),
        check_vma=False,
    )
```

```python
import jax
import jax.numpy as jnp
from jax import lax
from jax.experimental import pallas as pl
from jax.experimental.pallas import tpu as pltpu
from jax.sharding import PartitionSpec as P

T = 128
LEAD = 1024
NB = 8
RT = 6
CT = 12
ROWS = RT * T
COLS = CT * T
NZ = 8
ND = 5
MESH = pl.DeviceIdType.MESH
VMEM_LIMIT = 60 << 20
F32 = jnp.float32
BF16 = jnp.bfloat16
NN = (((1,), (0,)), ((), ()))
NT = (((1,), (1,)), ((), ()))
TN = (((0,), (0,)), ((), ()))


def dot1(a, b, dims):
    return lax.dot_general(a, b, dims, preferred_element_type=F32)


def split(a):
    hi = a.astype(BF16)
    return hi, (a - hi.astype(F32)).astype(BF16)


def dot3(a, b, dims):
    ah, al = split(a)
    bh, bl = split(b)
    return dot1(ah, bh, dims) + dot1(ah, bl, dims) + dot1(al, bh, dims)


def row_of(x, y):
    return y + jnp.where((x == 0) | (x == 3), 0, 4)


def panel_kernel(front, rm_ref, x_out, own_out, other_out,
                 ab, ra, rb, zs, u_ref, ub, ul, w_ref, dref, rbuf, wprev, xb, yb, upd, tmp, pr, pc, placed,
                 ga, gb, rows_f, rows_b, tile, rhalf,
                 lsem, s0, r0, sz, rz, sp, rp, sq, rq, sr, rr, st, rt, lt):
    team = lax.axis_index("team")
    pos = lax.axis_index("row")
    z = lax.axis_index("col")
    x, y = pos // 4, pos % 4
    xs = lambda d: ((x + d) % 4) * 4 + y
    ys = lambda d: x * 4 + (y + d) % 4
    row = row_of(x, y)

    c_col = pltpu.make_async_copy(front.at[0, :, pl.ds(0, T)], zs.at[z], lsem.at[0])
    c_row = pltpu.make_async_copy(front.at[0, pl.ds(0, T), :], rows_f, lsem.at[1])
    c_tile = pltpu.make_async_copy(front.at[0, pl.ds(0, T), pl.ds(0, T)], tile, lsem.at[2])
    c_tile.start()
    c_row.start()
    c_col.start()
    c_block = pltpu.make_async_copy(front.at[0], ab, lsem.at[8])
    c_out = pltpu.make_async_copy(xb, x_out, lsem.at[9])

    bar = pltpu.get_barrier_semaphore()
    for d in (1, 3):
        pl.semaphore_signal(bar, inc=1, device_id={"row": xs(d)}, device_id_type=MESH)
        pl.semaphore_signal(bar, inc=1, device_id={"row": ys(d)}, device_id_type=MESH)
    for d in range(1, NZ):
        pl.semaphore_signal(bar, inc=1, device_id={"col": (z + d) % NZ}, device_id_type=MESH)
    pl.semaphore_signal(bar, inc=1, device_id={"team": 1 - team}, device_id_type=MESH)
    for ref in (ub, ul, rbuf, wprev, xb, yb):
        ref[...] = jnp.zeros_like(ref)
    for d in range(1, NZ):
        pl.semaphore_signal(bar, inc=1, device_id={"row": (3 - x) * 4 + y, "col": (z + d) % NZ}, device_id_type=MESH)
    c_tile.wait()
    pl.semaphore_wait(bar, 4 + NZ + NZ - 1)

    mirror = {"row": (3 - x) * 4 + y}
    c1 = pltpu.make_async_remote_copy(rows_b.at[pl.ds(64, 64)], rhalf, s0.at[1], r0.at[1], device_id=mirror, device_id_type=MESH)

    def ring(step):
        up, dn = (z - step + 1 + NZ) % NZ, (z + step - 1) % NZ
        if step < 4:
            src_u, src_d = zs.at[up], zs.at[dn]
        else:
            src_u, src_d = zs.at[up, pl.ds(0, ROWS // 2)], zs.at[dn, pl.ds(ROWS // 2, ROWS // 2)]
        a = pltpu.make_async_remote_copy(src_u, src_u, sr.at[0, step - 1], rr.at[0, step - 1], device_id={"col": (z + 1) % NZ}, device_id_type=MESH)
        b = pltpu.make_async_remote_copy(src_d, src_d, sr.at[1, step - 1], rr.at[1, step - 1], device_id={"col": (z + NZ - 1) % NZ}, device_id_type=MESH)
        return a, b

    def ring_recv(step):
        up, dn = (z - step + NZ) % NZ, (z + step) % NZ
        if step < 4:
            dst_u, dst_d = zs.at[up], zs.at[dn]
        else:
            dst_u, dst_d = zs.at[up, pl.ds(0, ROWS // 2)], zs.at[dn, pl.ds(ROWS // 2, ROWS // 2)]
        pltpu.make_async_remote_copy(dst_u, dst_u, sr.at[0, step - 1], rr.at[0, step - 1], device_id={"col": (z + 1) % NZ}, device_id_type=MESH).wait_recv()
        pltpu.make_async_remote_copy(dst_d, dst_d, sr.at[1, step - 1], rr.at[1, step - 1], device_id={"col": (z + NZ - 1) % NZ}, device_id_type=MESH).wait_recv()

    mine = (z - row + NZ) % NZ
    slot = jnp.minimum(mine, ND - 1)
    lead_out = (x < 2) & (mine < ND)
    o1 = pltpu.make_async_copy(tile.at[pl.ds(0, 32)], ga.at[y, x, slot], lsem.at[4])
    o2 = pltpu.make_async_copy(tile.at[pl.ds(32, 32)], gb.at[x, y, slot], lsem.at[5])

    def zsend(k, d):
        px = x if k < 2 else 3 - x
        dst = ga.at[y, px, slot] if k % 2 == 0 else gb.at[px, y, slot]
        to = {"row": px * 4 + y, "col": (z + d) % NZ}
        return pltpu.make_async_remote_copy(tile.at[pl.ds(32 * k, 32)], dst, sz.at[k, d], rz.at[k % 2, slot], device_id=to, device_id_type=MESH)

    order = [(k, d) for d in (4, 3, 5, 2, 6, 1, 7, 0) for k in (2, 3, 0, 1) if d or k >= 2]

    @pl.when(lead_out)
    def _():
        for k, d in order:
            zsend(k, d).start()
        o1.start()
        o2.start()

    c_row.wait()
    rows_b[...] = rows_f[...].astype(BF16)
    for ref in (ub, ul, rbuf, wprev, xb, yb):
        ref[...] = jnp.zeros_like(ref)

    @pl.when(x < 2)
    def _():
        c1.start()

    @pl.when(lead_out)
    def _():
        o1.wait()
        o2.wait()

    for d in range(ND):
        @pl.when((mine != d) | (x >= 2))
        def _():
            pltpu.make_async_remote_copy(tile.at[pl.ds(0, 32)], ga.at[y, x, d], sz.at[0, 0], rz.at[0, d], device_id={"col": (z + 1) % NZ}, device_id_type=MESH).wait_recv()
            pltpu.make_async_remote_copy(tile.at[pl.ds(32, 32)], gb.at[x, y, d], sz.at[1, 0], rz.at[1, d], device_id={"col": (z + 1) % NZ}, device_id_type=MESH).wait_recv()

    c_col.wait()
    for c in ring(1):
        c.start()
    c_block.start()

    def plane(buf, first, step, up, ss, rs, cut):
        f, s = (x, y) if first else (y, x)
        fd, sd = (xs, ys) if first else (ys, xs)
        if step <= 2:
            base = lambda d: buf.at[s, (f + d) % 4]
            dev = fd
        else:
            base = lambda d: buf.at[(s + d) % 4]
            dev = sd
        me = step - 1
        if step % 2 == 1:
            src, rcv = base(0), base(3 if up else 1)
        else:
            src, rcv = base(3 if up else 1), base(2)
            src, rcv = cut(src, up, step), cut(rcv, up, step)
        k = 0 if up else 1
        to = {"row": dev(1 if up else 3)}
        send = pltpu.make_async_remote_copy(src, src, ss.at[me, k], rs.at[me, k], device_id=to, device_id_type=MESH)
        recv = pltpu.make_async_remote_copy(rcv, rcv, ss.at[me, k], rs.at[me, k], device_id=to, device_id_type=MESH)
        return send, recv

    def cut_lead(ref, up, step):
        h = pl.ds(0 if up else 16, 16)
        return ref.at[:, h] if step == 2 else ref.at[:, :, h]

    def plane_step(step, bufs, ss, rs, cut):
        out = []
        for part in range(2):
            for up in (True, False):
                out.append(plane(bufs[part], part == 0, step, up, ss.at[part], rs.at[part], cut))
        return out

    def own_rows():
        @pl.when(x >= 2)
        def _():
            c1.wait_recv()

        def put(src):
            a = pltpu.make_async_copy(src.at[pl.ds(0, 32)], ra.at[y, x], lsem.at[6])
            b = pltpu.make_async_copy(src.at[pl.ds(32, 32)], rb.at[x, y], lsem.at[7])
            a.start()
            b.start()
            a.wait()
            b.wait()

        @pl.when(x >= 2)
        def _():
            put(rhalf)

        @pl.when(x < 2)
        def _():
            put(rows_b)

    def strip(kind, off=0):
        out = []
        for part, buf in enumerate((ra, rb)):
            f, s, fd, sd = (x, y, xs, ys) if part == 0 else (y, x, ys, xs)
            spot = lambda ds, df: buf.at[(s + ds) % 4, (f + df) % 4]
            for k in range(2):
                h = pl.ds(16 * k, 16)
                back = 1 if k else 3
                src, dst = {
                    1: lambda: (spot(0, 0), spot(0, back)),
                    2: lambda: (spot(0, back).at[h], spot(0, 2).at[h]),
                    3: lambda: (spot(0, off), spot(back, off)),
                    4: lambda: (spot(back, off).at[h], spot(2, off).at[h]),
                }[kind]()
                to = {"row": (fd if kind < 3 else sd)(4 - back)}
                sem = (kind - 1) if kind < 3 else 2 + 4 * (kind - 3) + off
                out.append((
                    pltpu.make_async_remote_copy(src, src, sq.at[part, sem, k], rq.at[part, sem, k], device_id=to, device_id_type=MESH),
                    pltpu.make_async_remote_copy(dst, dst, sq.at[part, sem, k], rq.at[part, sem, k], device_id=to, device_id_type=MESH),
                ))
        return out

    def strip_start(*args):
        for s, _ in strip(*args):
            s.start()

    def strip_recv(*args):
        for _, r in strip(*args):
            r.wait_recv()

    def ring_start(step):
        for c in ring(step):
            c.start()

    for step in range(1, 5):
        cs = plane_step(step, (ga, gb), sp, rp, cut_lead)
        for s, _ in cs:
            s.start()
        if step == 3:
            ring_recv(1)
            ring_start(2)
        if step == 1:
            own_rows()
            one_hot(rm_ref, team, z, pc.at[0])
        elif step == 3:
            one_hot(rm_ref, team, z + NZ, pc.at[1])
            one_hot(rm_ref, team, pos, pr)
        for _, r in cs:
            r.wait_recv()

    def progress(J):
        @pl.when(J == 1)
        def _():
            strip_recv(1)
            strip_start(2)
            strip_start(3, 1)
            strip_start(3, 3)
            ring_recv(2)
            ring_start(3)

        @pl.when(J == 2)
        def _():
            strip_recv(2)
            strip_start(3, 2)
            strip_recv(3, 0)
            strip_start(4, 0)

        @pl.when(J == 3)
        def _():
            strip_recv(3, 1)
            strip_recv(3, 3)
            strip_start(4, 1)
            strip_start(4, 3)

        @pl.when(J == 4)
        def _():
            strip_recv(3, 2)
            strip_start(4, 2)
            ring_recv(3)
            ring_start(4)

    strip_start(1)
    strip_start(3, 0)
    assemble(ga, gb, u_ref)

    def ready():
        for off in range(4):
            strip_recv(4, off)

    def ring_ready():
        ring_recv(4)

    def pair_copies(c, n):
        ks = pl.ds(2 * n, 2)
        far = pltpu.make_async_remote_copy(placed.at[c, ks], other_out.at[c, ks], st.at[c, n], rt.at[c, n], device_id={"team": 1 - team}, device_id_type=MESH)
        near = pltpu.make_async_copy(placed.at[c, ks], own_out.at[c, ks], lt.at[c, n])
        return far, near

    pending = []

    def flush():
        for pair in pending:
            for copy in pair_copies(*pair):
                copy.start()
        pending.clear()

    def send(c, n):
        flush()
        pending.append((c, n))

    core(pos, ab, ra, rb, zs, u_ref, ub, ul, w_ref, dref, rbuf, wprev, xb, yb, upd, tmp, pr, pc, placed,
         progress, ready, ring_ready, c_block.wait, c_out.start, send)
    flush()

    for step in range(1, 5):
        for s, _ in plane_step(step, (ga, gb), sp, rp, cut_lead):
            s.wait_send()
        for c in ring(step):
            c.wait_send()

    for kind, off in [(1, 0), (2, 0)] + [(k, o) for k in (3, 4) for o in range(4)]:
        for s, _ in strip(kind, off):
            s.wait_send()

    for c in range(2):
        for n in range(3):
            far, near = pair_copies(c, n)
            far.wait()
            near.wait()
    c_out.wait()

    @pl.when(x < 2)
    def _():
        c1.wait_send()

    @pl.when(lead_out)
    def _():
        for k, d in order:
            zsend(k, d).wait_send()


def factor_block(block):
    sub = lax.broadcasted_iota(jnp.int32, (8, T), 0)
    lane = lax.broadcasted_iota(jnp.int32, (8, T), 1)
    V = [block[8 * s : 8 * s + 8, :] for s in range(16)]
    W = [jnp.where(lane == sub + 8 * s, 1.0, 0.0).astype(F32) for s in range(16)]
    lb = lambda v, j: jnp.broadcast_to(v[:, j : j + 1], (8, T))
    sb = lambda v, k: jnp.broadcast_to(v[k : k + 1, :], (8, T))
    for t in range(16):
        v, w = V[t], W[t]
        C = [lb(v, 8 * t + j) for j in range(8)]
        rv, rw, rs, uk = [], [], [], []
        for k in range(8):
            r = lax.rsqrt(sb(C[k], k))
            a, b = sb(v, k) * r, sb(w, k) * r
            m = jnp.where(sub > k, C[k] * r, 0.0)
            us = {}
            for j in range(k + 1, 8):
                us[j] = sb(C[j], k) * r
                C[j] = C[j] - m * us[j]
            v = jnp.where(sub == k, a, v - m * a)
            w = jnp.where(sub == k, b, w - m * b)
            rv.append(a)
            rw.append(b)
            rs.append(r)
            uk.append(us)
        V[t], W[t] = v, w
        for s in range(t + 1, 16):
            Cs = [lb(V[s], 8 * t + j) for j in range(8)]
            vs, ws = V[s], W[s]
            for k in range(8):
                m = Cs[k] * rs[k]
                for j in range(k + 1, 8):
                    Cs[j] = Cs[j] - m * uk[k][j]
                vs = vs - m * rv[k]
                ws = ws - m * rw[k]
            V[s], W[s] = vs, ws
    return jnp.concatenate(W, axis=0)


def assemble(ga, gb, u_ref):
    for i in range(NB):
        y = i % 4
        top, bot = (0, 3) if i < 4 else (1, 2)
        for d in range(ND):
            j = (i + d) % NB
            if d == 4 and i >= 4:
                continue
            parts = [ga[y, top, d], gb[top, y, d], ga[y, bot, d], gb[bot, y, d]]
            if j >= i:
                for k in range(4):
                    u_ref[i * T + 32 * k : i * T + 32 * k + 32, j * T : j * T + T] = parts[k]
            else:
                u_ref[j * T : j * T + T, i * T : i * T + T] = jnp.concatenate(parts, axis=0).T
    for i in range(1, NB):
        u_ref[i * T : i * T + T, 0 : i * T] = jnp.zeros((T, i * T), F32)


def at(J):
    return J * T if isinstance(J, int) else pl.multiple_of(J * T, T)


def lead_step(J, depth, c0, u_ref, uh, ul, w_ref, dref, rbuf, wprev, filler):
    fixed = isinstance(J, int)
    last = fixed and J == NB - 1
    wide = LEAD - c0
    cols = pl.ds(c0, wide)
    j0 = at(J)
    p0 = at(J - 1 if fixed else jnp.maximum(J - 1, 0))
    n0 = at(min(J + 1, NB - 1) if fixed else jnp.minimum(J + 1, NB - 1))
    col = lax.broadcasted_iota(jnp.int32, (T, wide), 1) + c0
    sub = lax.broadcasted_iota(jnp.int32, (T, wide), 0)
    filler()
    row = jnp.where(col >= sub + p0, dot3(wprev[...], rbuf[:, cols], NN), 0.0)
    hi, lo = split(row)
    uh[pl.ds(p0, T), cols] = hi
    ul[pl.ds(p0, T), cols] = lo

    def ahead(mine, them):
        mh, ml, th, tl = uh[:depth, mine], ul[:depth, mine], uh[:depth, them], ul[:depth, them]
        return dot1(mh, th, TN) + dot1(mh, tl, TN) + dot1(ml, th, TN)

    if not last:
        rbuf[:, cols] = u_ref[pl.ds(j0, T), cols] - ahead(pl.ds(j0, T), cols)
        nxt = u_ref[pl.ds(n0, T), pl.ds(n0, T)] - ahead(pl.ds(n0, T), pl.ds(n0, T))
    inv = factor_block(dref[...])
    w_ref[J] = inv
    if not last:
        wprev[...] = inv
        edge = dot3(inv, rbuf[:, pl.ds(n0, T)], NN)
        dref[...] = nxt - dot3(edge, edge, TN)


def one_hot(rm_ref, team, first, out):
    sub = lax.broadcasted_iota(jnp.int32, (ROWS, T), 0)
    for s in range(RT):
        tile = s * 16 + first
        both = rm_ref[:, pl.ds(pl.multiple_of(jnp.maximum(tile - NB, 0) * T, T), T)]
        line = jnp.where(team == 0, both[0:1], both[1:2])
        spot = jnp.where(tile >= NB, (line // 2048) * T + line % T, -1)
        out[:, s * T : s * T + T] = jnp.where(sub == spot, 1.0, 0.0).astype(BF16)


def solve_rows(J, pos, zs, ub, w_ref, xb):
    d = J * T
    cs = slice(d, d + T)
    acc = zs[J]
    if d:
        acc = acc - dot1(xb[:, :d], ub[:d, cs], NN)
    xj = dot3(acc, w_ref[J], NT)
    r = lax.broadcasted_iota(jnp.int32, (T, T), 0)
    c = lax.broadcasted_iota(jnp.int32, (T, T), 1)
    xb[T:, cs] = xj[T:].astype(BF16)
    xb[:T, cs] = jnp.where(pos * T + r >= d + c, xj[:T], 0.0).astype(BF16)


def solve_cols(J, ra, rb, ub, w_ref, yb):
    d = J * T
    cs = slice(d, d + T)
    y, top = J % 4, J // 4
    acc = jnp.concatenate([ra[y, top], rb[top, y], ra[y, 3 - top], rb[3 - top, y]], axis=0).astype(F32)
    if d:
        acc = acc - dot1(ub[:d, cs], yb[:d, :], TN)
    yb[cs, :] = dot3(w_ref[J], acc, NN).astype(BF16)


def place(pr, pc, upd, tmp, placed, send):
    for c in range(2):
        for n in range(3):
            tmp[c, n] = dot1(upd[c], pc[c, n * 256 : n * 256 + 256, :], NT).astype(BF16)
            out = dot1(pr[...], tmp[c, n], NN).astype(BF16)
            placed[c, 2 * n] = out[:, :T]
            placed[c, 2 * n + 1] = out[:, T:]
            send(c, n)


def core(pos, ab, ra, rb, zs, u_ref, ub, ul, w_ref, dref, rbuf, wprev, xb, yb, upd, tmp, pr, pc, placed, progress, ready, ring_ready, block_ready, solved, send):
    lead = (u_ref, ub, ul, w_ref, dref, rbuf, wprev)
    dref[...] = u_ref[:T, :T]

    def early(J, _):
        progress(J)
        lead_step(J, 4 * T, 0, *lead, lambda: None)
        return 0

    lax.fori_loop(0, 5, early, 0)
    rows = lambda *js: [solve_rows(j, pos, zs, ub, w_ref, xb) for j in js]
    columns = lambda *js: [solve_cols(j, ra, rb, ub, w_ref, yb) for j in js]
    ready()
    lead_step(5, 5 * T, 5 * T, *lead, lambda: columns(0, 1, 2, 3))
    ring_ready()
    lead_step(6, 6 * T, 5 * T, *lead, lambda: (rows(0, 1, 2, 3, 4, 5), columns(4, 5)))
    block_ready()

    def last():
        for n in range(6):
            cs = slice(n * 256, n * 256 + 256)
            ab[:, cs] = ab[:, cs] - dot1(xb[:, : 6 * T], yb[: 6 * T, cs], NN)
        rows(6)
        columns(6)

    lead_step(7, 7 * T, 6 * T, *lead, last)
    rows(7)
    columns(7)
    solved()
    for n in range(6):
        cs = slice(n * 256, n * 256 + 256)
        v = (ab[:, cs] - dot1(xb[:, 6 * T :], yb[6 * T :, cs], NN)).astype(BF16)
        upd[0, :, n * T : n * T + T] = v[:, :T]
        upd[1, :, n * T : n * T + T] = v[:, T:]
    place(pr, pc, upd, tmp, placed, send)


def panels(front, rm):
    vm = pl.BlockSpec(memory_space=pltpu.VMEM)
    hbm = pl.BlockSpec(memory_space=pl.ANY)
    dma = pltpu.SemaphoreType.DMA
    v = pltpu.VMEM
    return pl.pallas_call(
        panel_kernel,
        out_shape=(
            jax.ShapeDtypeStruct((ROWS, LEAD), BF16),
            jax.ShapeDtypeStruct((2, RT, ROWS, T), BF16),
            jax.ShapeDtypeStruct((2, RT, ROWS, T), BF16),
        ),
        in_specs=[hbm, vm],
        out_specs=(hbm,) * 3,
        scratch_shapes=[
            v((ROWS, COLS), F32), v((4, 4, 32, COLS), BF16), v((4, 4, 32, COLS), BF16), v((NZ, ROWS, T), F32),
            v((LEAD, LEAD), F32), v((LEAD, LEAD), BF16), v((LEAD, LEAD), BF16), v((NB, T, T), F32),
            v((T, T), F32), v((T, LEAD), F32), v((T, T), F32), v((ROWS, LEAD), BF16), v((LEAD, COLS), BF16),
            v((2, ROWS, ROWS), BF16), v((2, 3, ROWS, 256), BF16), v((ROWS, ROWS), BF16), v((2, ROWS, ROWS), BF16), v((2, RT, ROWS, T), BF16),
            v((4, 4, ND, 32, T), F32), v((4, 4, ND, 32, T), F32),
            v((T, COLS), F32), v((T, COLS), BF16), v((T, T), F32), v((64, COLS), BF16),
            dma((10,)), dma((2,)), dma((2,)), dma((4, NZ)), dma((2, ND)),
            dma((2, 4, 2)), dma((2, 4, 2)), dma((2, 10, 2)), dma((2, 10, 2)), dma((2, 4)), dma((2, 4)),
            dma((2, 3)), dma((2, 3)), dma((2, 3)),
        ],
        compiler_params=pltpu.CompilerParams(collective_id=0, has_side_effects=True, vmem_limit_bytes=VMEM_LIMIT),
        name="panels",
    )(front, rm)


def finish_kernel(owner_ref, own, other, xb, fac, out):
    team = lax.axis_index("team")
    pos = lax.axis_index("row")
    fac[0] = xb[...].astype(F32)
    for s in range(RT):
        keep = owner_ref[s * 16 + pos] == team
        rows = slice(s * T, s * T + T)
        for c in range(2):
            total = own[c, 0, rows].astype(F32) + other[c, 0, rows].astype(F32)
            out[0, rows, c * T : c * T + T] = jnp.where(keep, total, 0.0)


def finish(tile_owner, own, other, xb):
    tiles = pl.BlockSpec((2, 1, ROWS, T), lambda k: (0, k, 0, 0))
    return pl.pallas_call(
        finish_kernel,
        grid=(RT,),
        out_shape=(jax.ShapeDtypeStruct((1, ROWS, LEAD), F32), jax.ShapeDtypeStruct((1, ROWS, COLS), F32)),
        in_specs=[pl.BlockSpec(memory_space=pltpu.SMEM), tiles, tiles, pl.BlockSpec((T, LEAD), lambda k: (k, 0))],
        out_specs=(pl.BlockSpec((1, T, LEAD), lambda k: (0, k, 0)), pl.BlockSpec((1, ROWS, 2 * T), lambda k: (0, 0, k))),
        name="finish",
    )(tile_owner, own, other, xb)


def shards(front, row_map, tile_owner):
    xb, own, other = panels(front, row_map)
    return finish(tile_owner, own, other, xb)


def solution(mesh):
    return jax.shard_map(
        shards,
        mesh=mesh,
        in_specs=(P("team", "row", "col"), P(), P()),
        out_specs=(P("team", "row", None), P("team", "row", "col")),
        check_vma=False,
    )
```
